128 devices in a mesh: dom: 64 (over x, z, y), batch: 2 (over core).
Axes of the slice: x: 4, y: 4, z: 4, core: 2. Of those that a mesh axis runs over, the one named last changes fastest.
Arguments:
- features: bfloat16 [4, 65536, 512], P('batch', 'dom'), may hold values from -6 to 6
- tile_vals: bfloat16 [2048, 128, 128], P('dom'), may hold values from -0.25 to 0.25
- tile_row: int32 [2048], P('dom'), may hold values from 0 to 7
- tile_col: int32 [2048], P('dom'), may hold values from 0 to 11
- send_next: int32 [128], P('dom'), may hold values from 0 to 7
- send_prev: int32 [128], P('dom'), may hold values from 0 to 7
- cluster: int32 [65536], P('dom'), may hold values from 0 to 1023, as said below
- cotangent: bfloat16 [4, 65536, 512], P('batch', 'dom'), may hold values from -6 to 6
- self_weight: bfloat16 [512, 512], replicated, may hold values from -0.25 to 0.25
- neighbour_weight: bfloat16 [512, 512], replicated, may hold values from -0.25 to 0.25
- w_coarse: bfloat16 [512, 512], replicated, may hold values from -0.25 to 0.25
Outputs:
- output: bfloat16 [4, 65536, 512], P('batch', 'dom')
- self_weight_gradient: float32 [512, 512], replicated
- neighbour_weight_gradient: float32 [512, 512], replicated
- grad_coarse: float32 [512, 512], replicated
The draws below stay inside these ranges and needn't reach their ends.
Inputs may be any that keep to these rules, and one draw needn't show every extreme that they name: Within each pair of partitions 2m, 2m + 1, every cluster number names exactly two of the pair's 2 * 1024 nodes.
All inputs are finite; a program needn't handle non-finite values.
Results may differ from the reference program's by a relative error of at most 0.012.
Values may be sent and summed in bfloat16 or wider, within the bound.
A program may use at most 128 MiB of HBM per device.

```python
import math
import jax
import jax.numpy as jnp
from jax import lax

D = 512
BLK = 128
NODES_DEV = 1024
TILES_DEV = 32
HALO = 2
NB = 8
NODES = 65536
TILES = 2048
SENDS = 128
SCEN = 4
N_DOM = 64


def draw_cluster(key, part):
    pairs = NODES // (2 * NODES_DEV)
    keys = jax.random.split(jax.random.fold_in(key, 7), pairs)
    orders = jax.vmap(lambda single: jax.random.permutation(single, 2 * NODES_DEV))(keys)
    places = jnp.argsort(orders, axis=1, stable=True)
    return (places // 2).astype(jnp.int32).reshape(NODES)


def plant(entries, key, low, high):
    longest = entries.shape.index(max(entries.shape))
    spots = []
    for shift in (0, 1):
        where = [jax.random.randint(jax.random.fold_in(key, axis), (), 0, length) for axis, length in enumerate(entries.shape)]
        where[longest] = (where[longest] + shift) % entries.shape[longest]
        spots.append(tuple(where))
    return entries.at[spots[0]].set(low).at[spots[1]].set(high)


def block_scale(stream_key, shape, cuts, low, largest):
    gain = 1.0
    for axis_at, parts in cuts:
        heights = jax.random.uniform(jax.random.fold_in(jax.random.fold_in(stream_key, 6), axis_at), (parts,), jnp.float32, low / len(cuts), largest / len(cuts))
        gain = gain * jnp.repeat(jnp.exp(heights), shape[axis_at] // parts).reshape((-1,) + (1,) * (len(shape) - 1 - axis_at))
    return gain


def gaussian(own_key, dims, deviation, bound, cuts=(), kind=jnp.bfloat16):
    array = deviation * jax.random.normal(own_key, dims, jnp.float32)
    if cuts:
        array = array * block_scale(own_key, dims, cuts, -0.22, 0.18)
    return jnp.clip(array, -bound, bound).astype(kind)


def setup_inputs(seed: int = 0) -> dict:
    key_of = jax.random.split(jax.random.key(seed), 12)
    return {
        "features": gaussian(key_of[0], (SCEN, NODES, D), 1.0, 6.0, ((0, 2), (1, 64))),
        "tile_vals": gaussian(key_of[1], (TILES, BLK, BLK), (4 * BLK) ** -0.5, 0.25, ((0, 64),)),
        "tile_row": plant(jax.random.randint(key_of[2], (TILES,), 0, NB), jax.random.fold_in(key_of[2], 1), 0, NB - 1).astype(jnp.int32),
        "tile_col": plant(jax.random.randint(key_of[3], (TILES,), 0, NB + 2 * HALO), jax.random.fold_in(key_of[3], 1), 0, (NB + 2 * HALO) - 1).astype(jnp.int32),
        "send_next": plant(jax.random.randint(key_of[4], (SENDS,), 0, NB), jax.random.fold_in(key_of[4], 1), 0, NB - 1).astype(jnp.int32),
        "send_prev": plant(jax.random.randint(key_of[5], (SENDS,), 0, NB), jax.random.fold_in(key_of[5], 1), 0, NB - 1).astype(jnp.int32),
        "cluster": draw_cluster(jax.random.fold_in(key_of[11], 71), 0),
        "cotangent": gaussian(key_of[7], (SCEN, NODES, D), 1.0, 6.0, ((0, 2), (1, 64))),
        "self_weight": gaussian(key_of[8], (D, D), D ** -0.5, 0.25),
        "neighbour_weight": gaussian(key_of[9], (D, D), D ** -0.5, 0.25),
        "w_coarse": gaussian(key_of[10], (D, D), D ** -0.5, 0.25),
    }


def dsilu(value):
    sig = jax.nn.sigmoid(value)
    return sig * (1.0 + value * (1.0 - sig))

def matrix_product(form, left, right):
    return jnp.einsum(form, left.astype(jnp.float32), right.astype(jnp.float32), precision=lax.Precision.HIGHEST)

def reference(features, tile_vals, tile_row, tile_col, send_next, send_prev, cluster, cotangent, self_weight, neighbour_weight, w_coarse):
    blocks = features.reshape(SCEN, N_DOM, NB, BLK, D)
    tiles = tile_vals.reshape(N_DOM, TILES_DEV, BLK, BLK)
    rows_all = tile_row.reshape(N_DOM, TILES_DEV)
    cols_all = tile_col.reshape(N_DOM, TILES_DEV)
    nexts = send_next.reshape(N_DOM, HALO)
    prevs = send_prev.reshape(N_DOM, HALO)

    def one(part):
        local = blocks[:, part]
        before = jnp.maximum(part - 1, 0).astype(jnp.int32)
        after = jnp.minimum(part + 1, N_DOM - 1).astype(jnp.int32)
        got_prev = jnp.take(blocks[:, before], nexts[before], axis=1)
        got_prev = jnp.where(part > 0, got_prev, jnp.zeros_like(got_prev))
        got_next = jnp.take(blocks[:, after], prevs[after], axis=1)
        got_next = jnp.where(part < N_DOM - 1, got_next, jnp.zeros_like(got_next))
        extended = jnp.concatenate([local, got_prev, got_next], axis=1)
        picked = jnp.take(extended, cols_all[part], axis=1)
        terms = matrix_product('tij,stjd->stid', tiles[part], picked)
        rowhot = (rows_all[part][None, :] == jnp.arange(NB, dtype=jnp.int32)[:, None]).astype(jnp.float32)
        summed = jnp.einsum('rt,stid->srid', rowhot, terms, precision=lax.Precision.HIGHEST)
        return summed.astype(jnp.bfloat16)
    neighbour_total = lax.map(one, jnp.arange(N_DOM).astype(jnp.int32))
    neighbour_total = jnp.transpose(neighbour_total, (1, 0, 2, 3, 4)).reshape(SCEN, NODES, D)
    preactivation = matrix_product('jkb,bt->jkt', features, self_weight) + matrix_product('jkb,bt->jkt', neighbour_total, neighbour_weight)
    hidden = jax.nn.silu(preactivation).astype(jnp.bfloat16)
    index = (jnp.arange(NODES) // (2 * NODES_DEV) * NODES_DEV).astype(jnp.int32) + cluster
    count = NODES // 2
    sums = jax.ops.segment_sum(jnp.transpose(hidden.astype(jnp.float32), (1, 0, 2)), index, num_segments=count)
    coarse = (0.5 * sums).astype(jnp.bfloat16)
    act = matrix_product('ksd,de->kse', coarse, w_coarse)
    lifted = jax.nn.silu(act).astype(jnp.bfloat16)
    spread = jnp.transpose(jnp.take(lifted, index, axis=0), (1, 0, 2)).astype(jnp.float32)
    output = (hidden.astype(jnp.float32) + spread).astype(jnp.bfloat16)
    grad_lift = jax.ops.segment_sum(jnp.transpose(cotangent.astype(jnp.float32), (1, 0, 2)), index, num_segments=count)
    grad_act = (grad_lift * dsilu(act)).astype(jnp.bfloat16)
    gradient_scale = 1.0 / math.sqrt(SCEN * NODES)
    grad_coarse = matrix_product('ksd,kse->de', coarse, grad_act) * gradient_scale
    grad_down = matrix_product('kse,de->ksd', grad_act, w_coarse).astype(jnp.bfloat16)
    back = jnp.transpose(jnp.take(grad_down, index, axis=0), (1, 0, 2)).astype(jnp.float32)
    grad_hidden = cotangent.astype(jnp.float32) + 0.5 * back
    preactivation_gradient = (grad_hidden * dsilu(preactivation)).astype(jnp.bfloat16)
    self_weight_gradient = matrix_product('btv,btq->vq', features, preactivation_gradient) * gradient_scale
    neighbour_weight_gradient = matrix_product('btv,btq->vq', neighbour_total, preactivation_gradient) * gradient_scale
    return (output, self_weight_gradient, neighbour_weight_gradient, grad_coarse)
```

```python
import math

import jax
import jax.numpy as jnp
from jax import lax
from jax.experimental import pallas as pl
from jax.experimental.pallas import tpu as pltpu
from jax.sharding import PartitionSpec as P


def shifted(x, axis, by):
    length = lax.axis_size(axis)
    pairs = [(i, i + by) for i in range(length) if 0 <= i + by < length]
    return lax.ppermute(x, axis, pairs)


def partner(value, axis, distance):
    mask = 2**distance
    pairs = [(source, source ^ mask) for source in range(lax.axis_size(axis))]
    return lax.ppermute(value, axis, pairs)


def dsilu(value):
    sig = jax.nn.sigmoid(value)
    return sig * (1.0 + value * (1.0 - sig))


def member_table(labels, count):
    return (labels[None, :] == jnp.arange(count, dtype=jnp.int32)[:, None]).astype(jnp.bfloat16)


def pooling(rows, table):
    return jnp.einsum("cn,snd->scd", table, rows, preferred_element_type=jnp.float32)


def lookup(coarse_rows, table):
    return jnp.einsum("cn,scd->snd", table, coarse_rows, preferred_element_type=jnp.float32)


def pick_blocks(labels, count, tiled):
    table = (labels[:, None] == jnp.arange(count, dtype=jnp.int32)[None, :]).astype(jnp.bfloat16)
    return jnp.einsum("tb,sbjd->stjd", table, tiled, preferred_element_type=jnp.float32).astype(
        jnp.bfloat16
    )


MESH = pl.DeviceIdType.MESH
ORDERS = ((0, 1, 2), (1, 2, 0), (2, 0, 1))


def reduce_kernel(
    g0, g1, g2, out, send0, recv0, acc, buf1, recv1, sum2, buf2, recv2, sum3, buf3, recv3,
    send_sem, recv_sem, side_send, side_recv,
):
    gs = (g0, g1, g2)
    core = lax.axis_index("batch")
    dom = lax.axis_index("dom")
    where = (dom // 16, (dom // 4) % 4, dom % 4)
    weight = (16, 4, 1)

    def peer(axis, k):
        place = (where[axis] + k) % 4
        return (dom + (place - where[axis]) * weight[axis], core), place

    other = (dom, 1 - core)
    barrier = pltpu.get_barrier_semaphore()
    pl.semaphore_signal(barrier, inc=1, device_id=other, device_id_type=MESH)
    for axis in range(3):
        for k in (1, 2, 3):
            pl.semaphore_signal(barrier, inc=1, device_id=peer(axis, k)[0], device_id_type=MESH)
    for p in range(3):
        send0[p] = gs[p][1 - core].astype(jnp.bfloat16)
    pl.semaphore_wait(barrier, 10)

    first = []
    for p in range(3):
        copy = pltpu.make_async_remote_copy(
            src_ref=send0.at[p], dst_ref=recv0.at[p], send_sem=side_send.at[0, p],
            recv_sem=side_recv.at[0, p], device_id=other, device_id_type=MESH)
        copy.start()
        first.append(copy)

    def scatter(p, phase, pick, landing):
        copies = []
        for k in (1, 2, 3):
            device, place = peer(ORDERS[p][phase], k)
            copy = pltpu.make_async_remote_copy(
                src_ref=pick(place), dst_ref=landing.at[p, k - 1],
                send_sem=send_sem.at[phase, p, k - 1], recv_sem=recv_sem.at[phase, p, k - 1],
                device_id=device, device_id_type=MESH)
            copy.start()
            copies.append(copy)
        return copies

    def gather(p, phase, part):
        copies = []
        for k in (1, 2, 3):
            device, _ = peer(ORDERS[p][phase], k)
            copy = pltpu.make_async_remote_copy(
                src_ref=part, dst_ref=part,
                send_sem=send_sem.at[5 - phase, p, k - 1], recv_sem=recv_sem.at[5 - phase, p, k - 1],
                device_id=device, device_id_type=MESH)
            copy.start()
            copies.append(copy)
        return copies

    def mine(p, phase):
        return where[ORDERS[p][phase]]

    def cols(place):
        return pl.ds(pl.multiple_of(place * 128, 128), 128)

    pending = list(first)
    stage1 = []
    for p in range(3):
        first[p].wait_recv()
        total = gs[p][core] + recv0[p].astype(jnp.float32)
        acc[p] = total
        buf1[p] = total.astype(jnp.bfloat16)
        stage1.append(scatter(p, 0, lambda place: buf1.at[p, place], recv1))
    stage2 = []
    for p in range(3):
        for copy in stage1[p]:
            copy.wait_recv()
        total = acc[p, mine(p, 0)]
        for k in range(3):
            total = total + recv1[p, k].astype(jnp.float32)
        sum2[p] = total
        buf2[p] = total.astype(jnp.bfloat16)
        stage2.append(scatter(p, 1, lambda place: buf2.at[p, place], recv2))
    stage3 = []
    for p in range(3):
        for copy in stage2[p]:
            copy.wait_recv()
        total = sum2[p, mine(p, 1)]
        for k in range(3):
            total = total + recv2[p, k].astype(jnp.float32)
        sum3[p] = total
        buf3[p] = total.astype(jnp.bfloat16)
        stage3.append(scatter(p, 2, lambda place: buf3.at[p, :, cols(place)], recv3))
    stage4 = []
    for p in range(3):
        for copy in stage3[p]:
            copy.wait_recv()
        total = sum3[p, :, cols(mine(p, 2))]
        for k in range(3):
            total = total + recv3[p, k].astype(jnp.float32)
        part = out.at[p, core, mine(p, 0), mine(p, 1), :, cols(mine(p, 2))]
        part[...] = total.astype(jnp.bfloat16)
        stage4.append(gather(p, 2, part))
    stage5 = []
    for p in range(3):
        for copy in stage4[p]:
            copy.wait_recv()
        stage5.append(gather(p, 1, out.at[p, core, mine(p, 0), mine(p, 1)]))
    stage6 = []
    for p in range(3):
        for copy in stage5[p]:
            copy.wait_recv()
        stage6.append(gather(p, 0, out.at[p, core, mine(p, 0)]))
    last = []
    for p in range(3):
        for copy in stage6[p]:
            copy.wait_recv()
        copy = pltpu.make_async_remote_copy(
            src_ref=out.at[p, core], dst_ref=out.at[p, core], send_sem=side_send.at[1, p],
            recv_sem=side_recv.at[1, p], device_id=other, device_id_type=MESH)
        copy.start()
        last.append(copy)
    for copy in last:
        copy.wait_recv()
    for group in stage1 + stage2 + stage3 + stage4 + stage5 + stage6:
        for copy in group:
            copy.wait_send()
    for copy in first + last:
        copy.wait_send()


def reduce_all(parts):
    whole = pl.BlockSpec(memory_space=pltpu.VMEM)
    shaped = [part.reshape(2, 4, 4, 16, 512) for part in parts]
    half = (3, 4, 4, 16, 512)
    out = pl.pallas_call(
        reduce_kernel,
        out_shape=jax.ShapeDtypeStruct((3, 2, 4, 4, 16, 512), jnp.bfloat16),
        in_specs=[whole] * 3,
        out_specs=whole,
        scratch_shapes=[
            pltpu.VMEM(half, jnp.bfloat16),
            pltpu.VMEM(half, jnp.bfloat16),
            pltpu.VMEM(half, jnp.float32),
            pltpu.VMEM(half, jnp.bfloat16),
            pltpu.VMEM((3, 3, 4, 16, 512), jnp.bfloat16),
            pltpu.VMEM((3, 4, 16, 512), jnp.float32),
            pltpu.VMEM((3, 4, 16, 512), jnp.bfloat16),
            pltpu.VMEM((3, 3, 16, 512), jnp.bfloat16),
            pltpu.VMEM((3, 16, 512), jnp.float32),
            pltpu.VMEM((3, 16, 512), jnp.bfloat16),
            pltpu.VMEM((3, 3, 16, 128), jnp.bfloat16),
            pltpu.SemaphoreType.DMA((6, 3, 3)),
            pltpu.SemaphoreType.DMA((6, 3, 3)),
            pltpu.SemaphoreType.DMA((2, 3)),
            pltpu.SemaphoreType.DMA((2, 3)),
        ],
        compiler_params=pltpu.CompilerParams(
            collective_id=0, has_side_effects=True, vmem_limit_bytes=32 * 2**20
        ),
    )(*shaped)
    return out.reshape(3, 512, 512)


def local(
    features,
    tile_vals,
    tile_row,
    tile_col,
    send_next,
    send_prev,
    cluster,
    cotangent,
    self_weight,
    neighbour_weight,
    w_coarse,
):
    scen, nodes, width = features.shape
    side = tile_vals.shape[1]
    blocks = nodes // side
    tiled = features.reshape(scen, blocks, side, width)
    to_next = pick_blocks(send_next, blocks, tiled)
    to_prev = pick_blocks(send_prev, blocks, tiled)
    got_prev = shifted(to_next, "dom", 1)
    got_next = shifted(to_prev, "dom", -1)
    extended = jnp.concatenate([tiled, got_prev, got_next], axis=1)
    picked = pick_blocks(tile_col, extended.shape[1], extended)
    terms = jnp.einsum("tij,stjd->stid", tile_vals, picked, preferred_element_type=jnp.float32)
    rowhot = (tile_row[None, :] == jnp.arange(blocks, dtype=jnp.int32)[:, None]).astype(jnp.float32)
    summed = jnp.einsum("rt,stid->srid", rowhot, terms, precision=lax.Precision.HIGHEST)
    neighbour_total = summed.reshape(scen, nodes, width).astype(jnp.bfloat16)
    preactivation = jnp.einsum(
        "jkb,bt->jkt", features, self_weight, preferred_element_type=jnp.float32
    )
    preactivation = preactivation + jnp.einsum(
        "jkb,bt->jkt", neighbour_total, neighbour_weight, preferred_element_type=jnp.float32
    )
    hidden = jax.nn.silu(preactivation).astype(jnp.bfloat16)
    table = member_table(cluster, nodes)
    parity = lax.axis_index("dom") % 2
    half = nodes // 2
    own_start = parity * half

    def owned(array):
        return lax.dynamic_slice_in_dim(array, own_start, half, 1)

    partial_value = pooling(hidden, table)
    grad_partial = pooling(cotangent, table)
    partner_sums = partner(partial_value.astype(jnp.bfloat16), "dom", 0).astype(partial_value.dtype)
    coarse = (0.5 * (partial_value + partner_sums)).astype(jnp.bfloat16)
    act = jnp.einsum("skd,de->ske", coarse, w_coarse, preferred_element_type=jnp.float32)
    lifted = jax.nn.silu(act).astype(jnp.bfloat16)
    grad_lift = grad_partial + partner(grad_partial.astype(jnp.bfloat16), "dom", 0).astype(
        grad_partial.dtype
    )
    grad_act = (grad_lift * dsilu(act)).astype(jnp.bfloat16)
    term_coarse = jnp.einsum(
        "skd,ske->de", owned(coarse), owned(grad_act), preferred_element_type=jnp.float32
    )
    grad_down = jnp.einsum(
        "ske,de->skd", grad_act, w_coarse, preferred_element_type=jnp.float32
    ).astype(jnp.bfloat16)
    spread = lookup(lifted, table)
    output = (hidden.astype(jnp.float32) + spread).astype(jnp.bfloat16)
    back = lookup(grad_down, table)
    grad_hidden = cotangent.astype(jnp.float32) + 0.5 * back
    preactivation_gradient = (grad_hidden * dsilu(preactivation)).astype(jnp.bfloat16)
    self_contribution = jnp.einsum(
        "btv,btq->vq", features, preactivation_gradient, preferred_element_type=jnp.float32
    )
    neighbour_contribution = jnp.einsum(
        "btv,btq->vq", neighbour_total, preactivation_gradient, preferred_element_type=jnp.float32
    )
    totals = reduce_all((self_contribution, neighbour_contribution, term_coarse))
    totals = totals.astype(jnp.float32)
    gradient_scale = 1.0 / math.sqrt(scen * lax.axis_size("batch") * nodes * lax.axis_size("dom"))
    return (
        output,
        totals[0] * gradient_scale,
        totals[1] * gradient_scale,
        totals[2] * gradient_scale,
    )


def solution(mesh):
    in_specs = (
        P("batch", "dom", None),
        P("dom", None, None),
        P("dom"),
        P("dom"),
        P("dom"),
        P("dom"),
        P("dom"),
        P("batch", "dom", None),
        P(),
        P(),
        P(),
    )
    out_specs = (P("batch", "dom", None), P(), P(), P())
    return jax.shard_map(local, mesh=mesh, in_specs=in_specs, out_specs=out_specs, check_vma=False)
```

```python
import functools
import math

import jax
import jax.numpy as jnp
from jax import lax
from jax.experimental import pallas as pl
from jax.experimental.pallas import tpu as pltpu
from jax.sharding import PartitionSpec as P

N = 1024
D = 512
BLK = 128
NB = 8
SIDE = 2
LOW = 576
F32 = jnp.float32
BF16 = jnp.bfloat16
VM = pl.BlockSpec(memory_space=pltpu.VMEM)
SM = pl.BlockSpec(memory_space=pltpu.SMEM)


def shifted(x, axis, by):
    length = lax.axis_size(axis)
    pairs = [(i, i + by) for i in range(length) if 0 <= i + by < length]
    return lax.ppermute(x, axis, pairs)


def partner(value):
    pairs = [(source, source ^ 1) for source in range(lax.axis_size("dom"))]
    return lax.ppermute(value, "dom", pairs)


def silu_pair(value):
    sig = jax.nn.sigmoid(value)
    return value * sig, sig * (1.0 + value * (1.0 - sig))


def dot(left, right):
    return jnp.dot(left, right, preferred_element_type=F32)


def dot_tn(left, right):
    return lax.dot_general(left, right, (((0,), (0,)), ((), ())), preferred_element_type=F32)


def dot_nt(left, right):
    return lax.dot_general(left, right, (((1,), (1,)), ((), ())), preferred_element_type=F32)


def shape(*dims, dtype=BF16):
    return jax.ShapeDtypeStruct(dims, dtype)


def cost(flops, size):
    return pl.CostEstimate(flops=flops, bytes_accessed=size, transcendentals=0)


def pick_kernel(nexts, prevs, a_ref, b_ref, a_out, b_out):
    a_out[...] = a_ref[...]
    b_out[...] = b_ref[...]


def pick(nexts, prevs, tiled):
    block = (1, 1, BLK, D)
    return pl.pallas_call(
        pick_kernel,
        out_shape=(shape(SIDE, 2, BLK, D), shape(SIDE, 2, BLK, D)),
        grid_spec=pltpu.PrefetchScalarGridSpec(
            num_scalar_prefetch=2,
            grid=(SIDE, 2),
            in_specs=[
                pl.BlockSpec(block, lambda s, j, n, p: (s, n[j], 0, 0)),
                pl.BlockSpec(block, lambda s, j, n, p: (s, p[j], 0, 0)),
            ],
            out_specs=[pl.BlockSpec(block, lambda s, j, n, p: (s, j, 0, 0))] * 2,
        ),
        cost_estimate=cost(0, 2**21),
    )(nexts, prevs, tiled, tiled)


def store_split(value, low, high):
    low[...] = value[:LOW].astype(BF16)
    high[...] = value[LOW:].astype(BF16)


def label_kernel(row_ref, col_ref, ct_ref, lab_row, lab_col, count, low0, low1, high, table, flip):
    row, col = row_ref[...], col_ref[...]
    step = 256

    def tables(i, carry):
        at = pl.ds(pl.multiple_of(i * step, step), step)
        down = lax.broadcasted_iota(jnp.int32, (step, N), 0) + i * step
        across = lax.broadcasted_iota(jnp.int32, (step, N), 1)
        table[at, :] = (row == down).astype(F32).astype(BF16)
        flip[at, :] = (col_ref[at, :] == across).astype(F32).astype(BF16)
        return carry

    lax.fori_loop(0, N // step, tables, 0)
    held_row = dot(jnp.ones((16, N), BF16), flip[...])
    held_col = dot(table[...], jnp.ones((N, 128), BF16))

    def ones_of(held, value):
        return (held == value).astype(F32)

    total = jnp.sum(ones_of(held_row[:1], 1.0), axis=1, keepdims=True)
    row_in = jnp.concatenate([ones_of(held_row, 1.0), ones_of(held_row, 2.0)], axis=0).astype(BF16)
    col_in = jnp.concatenate([ones_of(held_col, 1.0), ones_of(held_col, 2.0)], axis=1).astype(BF16)

    def before(i, carry):
        at = pl.ds(pl.multiple_of(i * step, step), step)
        down = lax.broadcasted_iota(jnp.int32, (step, N), 0) + i * step
        across = lax.broadcasted_iota(jnp.int32, (step, N), 1)
        table[at, :] = (across < down).astype(F32).astype(BF16)
        flip[at, :] = (down < across).astype(F32).astype(BF16)
        return carry

    lax.fori_loop(0, N // step, before, 0)
    row_rank = dot(row_in, flip[...])
    col_rank = dot(table[...], col_in)
    new_row = jnp.where(held_row[:1] == 1.0, row_rank[:1], total + row_rank[16:17])
    new_col = jnp.where(held_col[:, :1] == 1.0, col_rank[:, :1], total + col_rank[:, 128:129])
    across = lax.broadcasted_iota(jnp.int32, (N, N), 1)
    down = lax.broadcasted_iota(jnp.int32, (N, N), 0)
    col_lab = jnp.sum(jnp.where(col == across, new_row, 0.0), axis=1, keepdims=True)
    row_lab = jnp.sum(jnp.where(row == down, new_col, 0.0), axis=0, keepdims=True)
    lab_col[...] = col_lab.astype(jnp.int32)
    lab_row[...] = row_lab.astype(jnp.int32)
    count[...] = jnp.broadcast_to(total, (8, 128)).astype(jnp.int32)
    table[...] = (row_lab.astype(jnp.int32) == down).astype(F32).astype(BF16)
    for s, low in ((0, low0), (1, low1)):
        store_split(dot(table[...], ct_ref[s]), low, high.at[s])


def label(cluster, cotangent):
    return pl.pallas_call(
        label_kernel,
        out_shape=(
            shape(1, N, dtype=jnp.int32),
            shape(N, 1, dtype=jnp.int32),
            shape(8, 128, dtype=jnp.int32),
            shape(LOW, D),
            shape(LOW, D),
            shape(SIDE, N - LOW, D),
        ),
        in_specs=[VM] * 3,
        out_specs=(VM,) * 6,
        scratch_shapes=[pltpu.VMEM((N, N), BF16), pltpu.VMEM((N, N), BF16)],
        compiler_params=pltpu.CompilerParams(vmem_limit_bytes=32 * 2**20),
        cost_estimate=cost(4 * 2**30, 2**22),
    )(cluster.reshape(1, N), cluster.reshape(N, 1), cotangent)


def node_kernel(
    rows, cols, lab_row, x_ref, prev_ref, next_ref, tiles, w_self, w_neigh,
    agg, hidden, slope, low0, low1, high, ext, acc, table,
):
    for s in range(SIDE):
        span = slice(s * D, (s + 1) * D)
        ext[0:NB, :, span] = x_ref[s].reshape(NB, BLK, D)
        ext[NB : NB + 2, :, span] = prev_ref[s]
        ext[NB + 2 : NB + 4, :, span] = next_ref[s]
    acc[...] = jnp.zeros_like(acc)

    def tile(t, carry):
        r = rows[t]
        acc[r] = acc[r] + dot(tiles[t], ext[cols[t]])
        return carry

    lax.fori_loop(0, tiles.shape[0], tile, 0)
    step = 256

    def block(i, carry):
        at = pl.ds(pl.multiple_of(i * step, step), step)
        down = lax.broadcasted_iota(jnp.int32, (step, N), 0) + i * step
        table[at, :] = (lab_row[...] == down).astype(F32).astype(BF16)
        for s in range(SIDE):
            span = slice(s * D, (s + 1) * D)
            got = acc[pl.ds(i * 2, 2), :, span].reshape(step, D).astype(BF16)
            agg[s, at, :] = got
            pre = dot(x_ref[s, at, :], w_self[...]) + dot(got, w_neigh[...])
            value, grad = silu_pair(pre)
            hidden[s, at, :] = value.astype(BF16)
            slope[s, at, :] = grad.astype(BF16)
        return carry

    lax.fori_loop(0, N // step, block, 0)
    for s, low in ((0, low0), (1, low1)):
        store_split(dot(table[...], hidden[s]), low, high.at[s])


def node_step(tile_row, tile_col, lab_row, features, got_prev, got_next, tiles, w_self, w_neigh):
    full = shape(SIDE, N, D)
    return pl.pallas_call(
        node_kernel,
        out_shape=(full, full, full, shape(LOW, D), shape(LOW, D), shape(SIDE, N - LOW, D)),
        in_specs=[SM, SM] + [VM] * 7,
        out_specs=(VM,) * 6,
        scratch_shapes=[
            pltpu.VMEM((NB + 4, BLK, SIDE * D), BF16),
            pltpu.VMEM((NB, BLK, SIDE * D), F32),
            pltpu.VMEM((N, N), BF16),
        ],
        compiler_params=pltpu.CompilerParams(vmem_limit_bytes=32 * 2**20),
        cost_estimate=cost(10 * 2**30, 2**23),
    )(tile_row, tile_col, lab_row, features, got_prev, got_next, tiles, w_self, w_neigh)


def tail_kernel(
    s, more, count, lab_col, rec_h, rec_c, far_h, far_c, low_h, high_h, low_c, high_c,
    hidden, slope, agg, x_ref, ct_ref, w_coarse, *rest,
):
    if more:
        old0, old1, old2, _, g0, g1, g2, out, flip, both = rest
    else:
        g0, g1, g2, out, flip, both = rest
    shared = lax.broadcasted_iota(jnp.int32, (N, 1), 0) < count[0:1, 0:1]

    def joined(low, high, rec, far):
        own = jnp.concatenate([low[...], high[s]], axis=0).astype(F32)
        got = jnp.concatenate([rec[...], far[s]], axis=0).astype(F32)
        return own + jnp.where(shared, got, 0.0)

    coarse = (0.5 * joined(low_h, high_h, rec_h, far_h)).astype(BF16)
    act = dot(coarse, w_coarse[...])
    value, grad = silu_pair(act)
    both[:, :D] = value.astype(BF16)
    grad_act = (joined(low_c, high_c, rec_c, far_c) * grad).astype(BF16)
    both[:, D:] = dot_nt(grad_act, w_coarse[...]).astype(BF16)
    weighed = (grad_act.astype(F32) * jnp.where(shared, 0.5, 1.0)).astype(BF16)
    third = dot_tn(coarse, weighed)
    across = lax.broadcasted_iota(jnp.int32, (N, N), 1)
    flip[...] = (lab_col[...] == across).astype(F32).astype(BF16)
    back = dot(flip[...], both[:, D:])
    grad_pre = ((ct_ref[s].astype(F32) + 0.5 * back) * slope[s].astype(F32)).astype(BF16)
    first = dot_tn(x_ref[s], grad_pre)
    second = dot_tn(agg[s], grad_pre)
    if more:
        g0[...] = old0[...] + first
        g1[...] = old1[...] + second
        g2[...] = old2[...] + third
    else:
        g0[...] = first
        g1[...] = second
        g2[...] = third
    out[0] = (hidden[s].astype(F32) + dot(flip[...], both[:, :D])).astype(BF16)


def tail(s, args, old):
    grads = (shape(D, D, dtype=F32),) * 3
    more = old is not None
    extra = list(old) if more else []
    return pl.pallas_call(
        functools.partial(tail_kernel, s, more),
        out_shape=grads + (shape(SIDE, N, D),),
        grid_spec=pl.GridSpec(
            grid=(1,),
            in_specs=[VM] * (len(args) + (3 if more else 0))
            + ([pl.BlockSpec(memory_space=pl.ANY)] if more else []),
            out_specs=(VM, VM, VM, pl.BlockSpec((1, N, D), lambda i: (s, 0, 0))),
            scratch_shapes=[pltpu.VMEM((N, N), BF16), pltpu.VMEM((N, 2 * D), BF16)],
        ),
        input_output_aliases={len(args) + 3: 3} if more else {},
        compiler_params=pltpu.CompilerParams(vmem_limit_bytes=40 * 2**20),
        cost_estimate=cost(8 * 2**30, 2**23),
    )(*args, *extra)


MESH = pl.DeviceIdType.MESH
ORDERS = ((0, 1, 2), (1, 2, 0), (2, 0, 1))


def reduce_kernel(
    g0, g1, g2, out, send0, recv0, acc, buf1, recv1, sum2, buf2, recv2, sum3, buf3, recv3,
    send_sem, recv_sem, side_send, side_recv,
):
    gs = (g0, g1, g2)
    core = lax.axis_index("batch")
    dom = lax.axis_index("dom")
    where = (dom // 16, (dom // 4) % 4, dom % 4)
    weight = (16, 4, 1)

    def peer(axis, k):
        place = (where[axis] + k) % 4
        return (dom + (place - where[axis]) * weight[axis], core), place

    other = (dom, 1 - core)
    barrier = pltpu.get_barrier_semaphore()
    pl.semaphore_signal(barrier, inc=1, device_id=other, device_id_type=MESH)
    for axis in range(3):
        for k in (1, 2, 3):
            pl.semaphore_signal(barrier, inc=1, device_id=peer(axis, k)[0], device_id_type=MESH)
    for p in range(3):
        send0[p] = gs[p][1 - core].astype(jnp.bfloat16)
    pl.semaphore_wait(barrier, 10)

    first = []
    for p in range(3):
        copy = pltpu.make_async_remote_copy(
            src_ref=send0.at[p], dst_ref=recv0.at[p], send_sem=side_send.at[0, p],
            recv_sem=side_recv.at[0, p], device_id=other, device_id_type=MESH)
        copy.start()
        first.append(copy)

    def scatter(p, phase, pick, landing):
        copies = []
        for k in (1, 2, 3):
            device, place = peer(ORDERS[p][phase], k)
            copy = pltpu.make_async_remote_copy(
                src_ref=pick(place), dst_ref=landing.at[p, k - 1],
                send_sem=send_sem.at[phase, p, k - 1], recv_sem=recv_sem.at[phase, p, k - 1],
                device_id=device, device_id_type=MESH)
            copy.start()
            copies.append(copy)
        return copies

    def gather(p, phase, part):
        copies = []
        for k in (1, 2, 3):
            device, _ = peer(ORDERS[p][phase], k)
            copy = pltpu.make_async_remote_copy(
                src_ref=part, dst_ref=part,
                send_sem=send_sem.at[5 - phase, p, k - 1], recv_sem=recv_sem.at[5 - phase, p, k - 1],
                device_id=device, device_id_type=MESH)
            copy.start()
            copies.append(copy)
        return copies

    def mine(p, phase):
        return where[ORDERS[p][phase]]

    def cols(place):
        return pl.ds(pl.multiple_of(place * 128, 128), 128)

    pending = list(first)
    stage1 = []
    for p in range(3):
        first[p].wait_recv()
        total = gs[p][core] + recv0[p].astype(jnp.float32)
        acc[p] = total
        buf1[p] = total.astype(jnp.bfloat16)
        stage1.append(scatter(p, 0, lambda place: buf1.at[p, place], recv1))
    stage2 = []
    for p in range(3):
        for copy in stage1[p]:
            copy.wait_recv()
        total = acc[p, mine(p, 0)]
        for k in range(3):
            total = total + recv1[p, k].astype(jnp.float32)
        sum2[p] = total
        buf2[p] = total.astype(jnp.bfloat16)
        stage2.append(scatter(p, 1, lambda place: buf2.at[p, place], recv2))
    stage3 = []
    for p in range(3):
        for copy in stage2[p]:
            copy.wait_recv()
        total = sum2[p, mine(p, 1)]
        for k in range(3):
            total = total + recv2[p, k].astype(jnp.float32)
        sum3[p] = total
        buf3[p] = total.astype(jnp.bfloat16)
        stage3.append(scatter(p, 2, lambda place: buf3.at[p, :, cols(place)], recv3))
    stage4 = []
    for p in range(3):
        for copy in stage3[p]:
            copy.wait_recv()
        total = sum3[p, :, cols(mine(p, 2))]
        for k in range(3):
            total = total + recv3[p, k].astype(jnp.float32)
        part = out.at[p, core, mine(p, 0), mine(p, 1), :, cols(mine(p, 2))]
        part[...] = total.astype(jnp.bfloat16)
        stage4.append(gather(p, 2, part))
    stage5 = []
    for p in range(3):
        for copy in stage4[p]:
            copy.wait_recv()
        stage5.append(gather(p, 1, out.at[p, core, mine(p, 0), mine(p, 1)]))
    stage6 = []
    for p in range(3):
        for copy in stage5[p]:
            copy.wait_recv()
        stage6.append(gather(p, 0, out.at[p, core, mine(p, 0)]))
    last = []
    for p in range(3):
        for copy in stage6[p]:
            copy.wait_recv()
        copy = pltpu.make_async_remote_copy(
            src_ref=out.at[p, core], dst_ref=out.at[p, core], send_sem=side_send.at[1, p],
            recv_sem=side_recv.at[1, p], device_id=other, device_id_type=MESH)
        copy.start()
        last.append(copy)
    for copy in last:
        copy.wait_recv()
    for group in stage1 + stage2 + stage3 + stage4 + stage5 + stage6:
        for copy in group:
            copy.wait_send()
    for copy in first + last:
        copy.wait_send()


def reduce_all(parts):
    whole = pl.BlockSpec(memory_space=pltpu.VMEM)
    shaped = [part.reshape(2, 4, 4, 16, 512) for part in parts]
    half = (3, 4, 4, 16, 512)
    out = pl.pallas_call(
        reduce_kernel,
        out_shape=jax.ShapeDtypeStruct((3, 2, 4, 4, 16, 512), jnp.bfloat16),
        in_specs=[whole] * 3,
        out_specs=whole,
        scratch_shapes=[
            pltpu.VMEM(half, jnp.bfloat16),
            pltpu.VMEM(half, jnp.bfloat16),
            pltpu.VMEM(half, jnp.float32),
            pltpu.VMEM(half, jnp.bfloat16),
            pltpu.VMEM((3, 3, 4, 16, 512), jnp.bfloat16),
            pltpu.VMEM((3, 4, 16, 512), jnp.float32),
            pltpu.VMEM((3, 4, 16, 512), jnp.bfloat16),
            pltpu.VMEM((3, 3, 16, 512), jnp.bfloat16),
            pltpu.VMEM((3, 16, 512), jnp.float32),
            pltpu.VMEM((3, 16, 512), jnp.bfloat16),
            pltpu.VMEM((3, 3, 16, 128), jnp.bfloat16),
            pltpu.SemaphoreType.DMA((6, 3, 3)),
            pltpu.SemaphoreType.DMA((6, 3, 3)),
            pltpu.SemaphoreType.DMA((2, 3)),
            pltpu.SemaphoreType.DMA((2, 3)),
        ],
        compiler_params=pltpu.CompilerParams(
            collective_id=0, has_side_effects=True, vmem_limit_bytes=32 * 2**20
        ),
    )(*shaped)
    return out.reshape(3, 512, 512)


def local(
    features,
    tile_vals,
    tile_row,
    tile_col,
    send_next,
    send_prev,
    cluster,
    cotangent,
    self_weight,
    neighbour_weight,
    w_coarse,
):
    to_next, to_prev = pick(send_next, send_prev, features.reshape(SIDE, NB, BLK, D))
    got_prev = shifted(to_next, "dom", 1)
    got_next = shifted(to_prev, "dom", -1)
    lab_row, lab_col, count, low_c0, low_c1, high_c = label(cluster, cotangent)
    most = lax.pmax(count[0, 0], ("dom", "batch"))
    rec_c0 = partner(low_c0)
    rec_c1 = partner(low_c1)
    agg, hidden, slope, low_h0, low_h1, high_h = node_step(
        tile_row, tile_col, lab_row, features, got_prev, got_next, tile_vals,
        self_weight, neighbour_weight,
    )
    rec_h0 = partner(low_h0)
    rec_h1 = partner(low_h1)
    far_h, far_c = lax.cond(
        most > LOW,
        lambda h, c: (partner(h), partner(c)),
        lambda h, c: (jnp.zeros_like(h), jnp.zeros_like(c)),
        high_h,
        high_c,
    )
    rest = (hidden, slope, agg, features, cotangent, w_coarse)
    old = tail(
        0, (count, lab_col, rec_h0, rec_c0, far_h, far_c, low_h0, high_h, low_c0, high_c) + rest, None
    )
    *grads, output = tail(
        1, (count, lab_col, rec_h1, rec_c1, far_h, far_c, low_h1, high_h, low_c1, high_c) + rest, old
    )
    totals = reduce_all(grads).astype(F32)
    scale = 1.0 / math.sqrt(SIDE * lax.axis_size("batch") * N * lax.axis_size("dom"))
    return output, totals[0] * scale, totals[1] * scale, totals[2] * scale


def solution(mesh):
    in_specs = (
        P("batch", "dom", None),
        P("dom", None, None),
        P("dom"),
        P("dom"),
        P("dom"),
        P("dom"),
        P("dom"),
        P("batch", "dom", None),
        P(),
        P(),
        P(),
    )
    out_specs = (P("batch", "dom", None), P(), P(), P())
    return jax.shard_map(local, mesh=mesh, in_specs=in_specs, out_specs=out_specs, check_vma=False)
```

```python
import math

import jax
import jax.numpy as jnp
from jax import lax
from jax.experimental import pallas as pl
from jax.experimental.pallas import tpu as pltpu
from jax.sharding import PartitionSpec as P

N = 1024
D = 512
BLK = 128
NB = 8
SIDE = 2
LOW = 576
F32 = jnp.float32
BF16 = jnp.bfloat16
VM = pl.BlockSpec(memory_space=pltpu.VMEM)
MESH = pl.DeviceIdType.MESH
SM = pl.BlockSpec(memory_space=pltpu.SMEM)


def partner(value):
    pairs = [(source, source ^ 1) for source in range(lax.axis_size("dom"))]
    return lax.ppermute(value, "dom", pairs)


def silu_pair(value):
    sig = jax.nn.sigmoid(value)
    return value * sig, sig * (1.0 + value * (1.0 - sig))


def dot(left, right):
    return jnp.dot(left, right, preferred_element_type=F32)


def dot_tn(left, right):
    return lax.dot_general(left, right, (((0,), (0,)), ((), ())), preferred_element_type=F32)


def dot_nt(left, right):
    return lax.dot_general(left, right, (((1,), (1,)), ((), ())), preferred_element_type=F32)


def shape(*dims, dtype=BF16):
    return jax.ShapeDtypeStruct(dims, dtype)


def cost(flops, size):
    return pl.CostEstimate(flops=flops, bytes_accessed=size, transcendentals=0)


class Place:
    def __init__(self):
        self.dom = lax.axis_index("dom")
        self.core = lax.axis_index("batch")
        self.at = (self.dom // 16, (self.dom // 4) % 4, self.dom % 4)

    def peer(self, axis, k):
        spot = (self.at[axis] + k) % 4
        return (self.dom + (spot - self.at[axis]) * (16, 4, 1)[axis], self.core), spot


def remote(src, dst, send, recv, device):
    copy = pltpu.make_async_remote_copy(
        src_ref=src, dst_ref=dst, send_sem=send, recv_sem=recv, device_id=device, device_id_type=MESH
    )
    copy.start()
    return copy


def greet(devices):
    barrier = pltpu.get_barrier_semaphore()
    for device in devices:
        pl.semaphore_signal(barrier, inc=1, device_id=device, device_id_type=MESH)
    return lambda: pl.semaphore_wait(barrier, len(devices))


def front_kernel(
    nexts, prevs, row_ref, col_ref, x_ref, ct_ref,
    lab_row, lab_col, count, most, sums, low, got_prev, got_next,
    to_next, to_prev, table, flip, peak, peaks,
    halo_send, halo_recv, peak_send, peak_recv,
):
    here = Place()
    nxt = ((here.dom + 1) % 64, here.core)
    prv = ((here.dom + 63) % 64, here.core)
    wait = greet([nxt, prv] + [here.peer(a, k)[0] for a in range(3) for k in (1, 2, 3)])
    for s in range(SIDE):
        for j in range(2):
            to_next[s, j] = x_ref[s, nexts[j]]
            to_prev[s, j] = x_ref[s, prevs[j]]
    wait()
    halo = []
    for s in range(SIDE):
        halo.append(remote(to_next.at[s], got_prev.at[s], halo_send.at[0, s], halo_recv.at[0, s], nxt))
        halo.append(remote(to_prev.at[s], got_next.at[s], halo_send.at[1, s], halo_recv.at[1, s], prv))

    row, col = row_ref[...], col_ref[...]
    step = 256

    def tables(i, carry):
        at = pl.ds(pl.multiple_of(i * step, step), step)
        down = lax.broadcasted_iota(jnp.int32, (step, N), 0) + i * step
        across = lax.broadcasted_iota(jnp.int32, (step, N), 1)
        table[at, :] = (row == down).astype(F32).astype(BF16)
        flip[at, :] = (col_ref[at, :] == across).astype(F32).astype(BF16)
        return carry

    lax.fori_loop(0, N // step, tables, 0)
    held_row = dot(jnp.ones((16, N), BF16), flip[...])
    held_col = dot(table[...], jnp.ones((N, 128), BF16))

    def ones_of(held, value):
        return (held == value).astype(F32)

    total = jnp.sum(ones_of(held_row[:1], 1.0), axis=1, keepdims=True)
    count[...] = jnp.broadcast_to(total, (8, 128)).astype(jnp.int32)
    peak[0] = jnp.broadcast_to(total, (8, 128))

    def spread(a):
        return [
            remote(peak.at[a], peaks.at[a, k - 1], peak_send.at[a, k - 1], peak_recv.at[a, k - 1], here.peer(a, k)[0])
            for k in (1, 2, 3)
        ]

    def settle(a, copies):
        for copy in copies:
            copy.wait()
        top = peak[a]
        for k in range(3):
            top = jnp.maximum(top, peaks[a, k])
        return top

    first = spread(0)
    row_in = jnp.concatenate([ones_of(held_row, 1.0), ones_of(held_row, 2.0)], axis=0).astype(BF16)
    col_in = jnp.concatenate([ones_of(held_col, 1.0), ones_of(held_col, 2.0)], axis=1).astype(BF16)

    def before(i, carry):
        at = pl.ds(pl.multiple_of(i * step, step), step)
        down = lax.broadcasted_iota(jnp.int32, (step, N), 0) + i * step
        across = lax.broadcasted_iota(jnp.int32, (step, N), 1)
        table[at, :] = (across < down).astype(F32).astype(BF16)
        flip[at, :] = (down < across).astype(F32).astype(BF16)
        return carry

    lax.fori_loop(0, N // step, before, 0)
    row_rank = dot(row_in, flip[...])
    col_rank = dot(table[...], col_in)
    new_row = jnp.where(held_row[:1] == 1.0, row_rank[:1], total + row_rank[16:17])
    new_col = jnp.where(held_col[:, :1] == 1.0, col_rank[:, :1], total + col_rank[:, 128:129])
    across = lax.broadcasted_iota(jnp.int32, (N, N), 1)
    down = lax.broadcasted_iota(jnp.int32, (N, N), 0)
    col_lab = jnp.sum(jnp.where(col == across, new_row, 0.0), axis=1, keepdims=True)
    row_lab = jnp.sum(jnp.where(row == down, new_col, 0.0), axis=0, keepdims=True)
    lab_col[...] = col_lab.astype(jnp.int32)
    lab_row[...] = row_lab.astype(jnp.int32)
    peak[1] = settle(0, first)
    second = spread(1)
    table[...] = (row_lab.astype(jnp.int32) == down).astype(F32).astype(BF16)

    def pool(s):
        got = dot(table[...], ct_ref[s]).astype(BF16)
        sums[s] = got
        low[s] = got[:LOW]

    pool(0)
    peak[2] = settle(1, second)
    third = spread(2)
    pool(1)
    most[...] = settle(2, third).astype(jnp.int32)
    for copy in halo:
        copy.wait()

    @pl.when(here.dom == 0)
    def _():
        got_prev[...] = jnp.zeros_like(got_prev)

    @pl.when(here.dom == 63)
    def _():
        got_next[...] = jnp.zeros_like(got_next)


def front(send_next, send_prev, cluster, features, cotangent):
    halo = (SIDE, 2, BLK, D)
    return pl.pallas_call(
        front_kernel,
        out_shape=(
            shape(1, N, dtype=jnp.int32),
            shape(N, 1, dtype=jnp.int32),
            shape(8, 128, dtype=jnp.int32),
            shape(8, 128, dtype=jnp.int32),
            shape(SIDE, N, D),
            shape(SIDE, LOW, D),
            shape(*halo),
            shape(*halo),
        ),
        in_specs=[SM, SM] + [VM] * 4,
        out_specs=(VM,) * 8,
        scratch_shapes=[
            pltpu.VMEM(halo, BF16),
            pltpu.VMEM(halo, BF16),
            pltpu.VMEM((N, N), BF16),
            pltpu.VMEM((N, N), BF16),
            pltpu.VMEM((3, 8, 128), F32),
            pltpu.VMEM((3, 3, 8, 128), F32),
            pltpu.SemaphoreType.DMA((2, SIDE)),
            pltpu.SemaphoreType.DMA((2, SIDE)),
            pltpu.SemaphoreType.DMA((3, 3)),
            pltpu.SemaphoreType.DMA((3, 3)),
        ],
        compiler_params=pltpu.CompilerParams(
            collective_id=0, has_side_effects=True, vmem_limit_bytes=28 * 2**20
        ),
        cost_estimate=cost(4 * 2**30, 2**22),
    )(
        send_next, send_prev, cluster.reshape(1, N), cluster.reshape(N, 1),
        features.reshape(SIDE, NB, BLK, D), cotangent,
    )


def node_kernel(
    rows, cols, lab_row, x_ref, prev_ref, next_ref, tiles, w_self, w_neigh,
    agg, hidden, slope, sums, ext, acc, table,
):
    for s in range(SIDE):
        span = slice(s * D, (s + 1) * D)
        ext[0:NB, :, span] = x_ref[s].reshape(NB, BLK, D)
        ext[NB : NB + 2, :, span] = prev_ref[s]
        ext[NB + 2 : NB + 4, :, span] = next_ref[s]
    acc[...] = jnp.zeros_like(acc)

    def tile(t, carry):
        r = rows[t]
        acc[r] = acc[r] + dot(tiles[t], ext[cols[t]])
        return carry

    lax.fori_loop(0, tiles.shape[0], tile, 0)
    step = 256

    def block(i, carry):
        at = pl.ds(pl.multiple_of(i * step, step), step)
        down = lax.broadcasted_iota(jnp.int32, (step, N), 0) + i * step
        table[at, :] = (lab_row[...] == down).astype(F32).astype(BF16)
        for s in range(SIDE):
            span = slice(s * D, (s + 1) * D)
            got = acc[pl.ds(i * 2, 2), :, span].reshape(step, D).astype(BF16)
            agg[s, at, :] = got
            pre = dot(x_ref[s, at, :], w_self[...]) + dot(got, w_neigh[...])
            value, grad = silu_pair(pre)
            hidden[s, at, :] = value.astype(BF16)
            slope[s, at, :] = grad.astype(BF16)
        return carry

    lax.fori_loop(0, N // step, block, 0)
    for s in range(SIDE):
        sums[s] = dot(table[...], hidden[s]).astype(BF16)


def node_step(tile_row, tile_col, lab_row, features, got_prev, got_next, tiles, w_self, w_neigh):
    full = shape(SIDE, N, D)
    return pl.pallas_call(
        node_kernel,
        out_shape=(full,) * 4,
        in_specs=[SM, SM] + [VM] * 7,
        out_specs=(VM,) * 4,
        scratch_shapes=[
            pltpu.VMEM((NB + 4, BLK, SIDE * D), BF16),
            pltpu.VMEM((NB, BLK, SIDE * D), F32),
            pltpu.VMEM((N, N), BF16),
        ],
        compiler_params=pltpu.CompilerParams(vmem_limit_bytes=24 * 2**20),
        cost_estimate=cost(10 * 2**30, 2**23),
    )(tile_row, tile_col, lab_row, features, got_prev, got_next, tiles, w_self, w_neigh)


EARLY, MID, LAST = (640, 1024), (0, 384), (384, 640)
ORDERS = ((0, 1, 2), (1, 2, 0), (2, 0, 1))
ENTRY = (2, 0, 1)


def back_kernel(
    count, lab_col, sums_h, sums_c, rec_c, far_h, far_c, hidden, slope, agg, x_ref, ct_ref, w_coarse,
    total, out,
    rec_h, flip, lifted, down, coarse, weighed, x_turn, a_turn, w_turn, grad_pre, part, grads,
    send0, recv0, acc, buf1, recv1, sum2, buf2, recv2, sum3, buf3, recv3,
    swap_send, swap_recv, send_sem, recv_sem, side_send, side_recv,
):
    here = Place()
    core = here.core
    other = (here.dom, 1 - core)
    pair = (here.dom + 1 - 2 * (here.dom % 2), core)
    wait = greet([other, pair] + [here.peer(a, k)[0] for a in range(3) for k in (1, 2, 3)])
    wait()
    swaps = []
    for s in range(SIDE):
        for i, (lo, hi) in enumerate((MID, (LAST[0], LOW))):
            rows = pl.ds(lo, hi - lo)
            swaps.append(
                remote(sums_h.at[s, rows], rec_h.at[s, rows], swap_send.at[s, i], swap_recv.at[s, i], pair)
            )

    step = 256

    def one_hot(i, carry):
        at = pl.ds(pl.multiple_of(i * step, step), step)
        across = lax.broadcasted_iota(jnp.int32, (step, N), 1)
        flip[at, :] = (lab_col[at, :] == across).astype(F32).astype(BF16)
        return carry

    lax.fori_loop(0, N // step, one_hot, 0)
    w_turn[...] = w_coarse[...].T

    def level(s, span):
        lo, hi = span
        shared = lax.broadcasted_iota(jnp.int32, (hi - lo, 1), 0) + lo < count[0:1, 0:1]

        def joined(own, rec, far):
            if lo >= LOW:
                got = far[s, lo - LOW : hi - LOW]
            elif hi <= LOW:
                got = rec[s, lo:hi]
            else:
                got = jnp.concatenate([rec[s, lo:LOW], far[s, : hi - LOW]], axis=0)
            return own[s, lo:hi].astype(F32) + jnp.where(shared, got.astype(F32), 0.0)

        rows = (0.5 * joined(sums_h, rec_h, far_h)).astype(BF16)
        coarse[s, lo:hi] = rows
        value, grad = silu_pair(dot(rows, w_coarse[...]))
        lifted[s, lo:hi] = value.astype(BF16)
        grad_act = (joined(sums_c, rec_c, far_c) * grad).astype(BF16)
        down[s, lo:hi] = dot(grad_act, w_turn[...]).astype(BF16)
        weighed[s, lo:hi] = (grad_act.astype(F32) * jnp.where(shared, 0.5, 1.0)).astype(BF16)

    def looked(s, span):
        lo, hi = span
        return dot(flip[:, lo:hi], down[s, lo:hi])

    def product(s, span):
        lo, hi = span
        return dot_tn(coarse[s, lo:hi], weighed[s, lo:hi])

    def emit(s, lo, hi):
        out[s, lo:hi] = (hidden[s, lo:hi].astype(F32) + dot(flip[lo:hi, :], lifted[s])).astype(BF16)

    def store(p, value):
        grads[p] = value.reshape(2, 4, 4, 16, D)

    def load(p):
        return grads[p].reshape(D, D)

    for s in range(SIDE):
        level(s, EARLY)
        x_turn[s] = x_ref[s].T
        a_turn[s] = agg[s].T

    swaps[0].wait_recv()
    level(0, MID)
    swaps[1].wait_recv()
    level(0, LAST)
    back = dot(flip[...], down[0])
    grad_pre[...] = ((ct_ref[0].astype(F32) + 0.5 * back) * slope[0].astype(F32)).astype(BF16)
    store(0, dot(x_turn[0], grad_pre[...]))
    store(1, dot(a_turn[0], grad_pre[...]))
    store(2, product(0, (0, N)) + product(1, EARLY))
    part[...] = looked(1, EARLY)
    emit(0, 0, N)

    swaps[2].wait_recv()
    level(1, MID)
    part[...] += looked(1, MID)
    store(2, load(2) + product(1, MID))
    swaps[3].wait_recv()
    level(1, LAST)
    first = [None] * 3

    def hand(p):
        send0[p] = grads[p, 1 - core].astype(BF16)
        first[p] = remote(send0.at[p], recv0.at[p], side_send.at[0, p], side_recv.at[0, p], other)

    store(2, load(2) + product(1, LAST))
    hand(2)
    back = part[...] + looked(1, LAST)
    grad_pre[...] = ((ct_ref[1].astype(F32) + 0.5 * back) * slope[1].astype(F32)).astype(BF16)
    store(0, load(0) + dot(x_turn[1], grad_pre[...]))
    hand(0)
    store(1, load(1) + dot(a_turn[1], grad_pre[...]))
    hand(1)

    def scatter(p, phase, pick, landing):
        copies = []
        for k in (1, 2, 3):
            device, spot = here.peer(ORDERS[p][phase], k)
            copies.append(
                remote(
                    pick(spot), landing.at[p, k - 1], send_sem.at[phase, p, k - 1],
                    recv_sem.at[phase, p, k - 1], device,
                )
            )
        return copies

    def gather(p, phase, piece):
        return [
            remote(
                piece, piece, send_sem.at[5 - phase, p, k - 1], recv_sem.at[5 - phase, p, k - 1],
                here.peer(ORDERS[p][phase], k)[0],
            )
            for k in (1, 2, 3)
        ]

    def mine(p, phase):
        return here.at[ORDERS[p][phase]]

    def cols(spot):
        return pl.ds(pl.multiple_of(spot * 128, 128), 128)

    stages = [[None] * 3 for _ in range(6)]

    def arrived(stage, p):
        for copy in stages[stage][p]:
            copy.wait_recv()

    for p in ENTRY:
        first[p].wait_recv()
        value = grads[p, core] + recv0[p].astype(F32)
        acc[p] = value
        buf1[p] = value.astype(BF16)
        stages[0][p] = scatter(p, 0, lambda spot: buf1.at[p, spot], recv1)
    emit(1, 0, 512)
    for p in ENTRY:
        arrived(0, p)
        value = acc[p, mine(p, 0)]
        for k in range(3):
            value = value + recv1[p, k].astype(F32)
        sum2[p] = value
        buf2[p] = value.astype(BF16)
        stages[1][p] = scatter(p, 1, lambda spot: buf2.at[p, spot], recv2)
    emit(1, 512, 768)
    for p in ENTRY:
        arrived(1, p)
        value = sum2[p, mine(p, 1)]
        for k in range(3):
            value = value + recv2[p, k].astype(F32)
        sum3[p] = value
        buf3[p] = value.astype(BF16)
        stages[2][p] = scatter(p, 2, lambda spot: buf3.at[p, :, cols(spot)], recv3)
    emit(1, 768, 1024)
    for p in ENTRY:
        arrived(2, p)
        value = sum3[p, :, cols(mine(p, 2))]
        for k in range(3):
            value = value + recv3[p, k].astype(F32)
        piece = total.at[p, core, mine(p, 0), mine(p, 1), :, cols(mine(p, 2))]
        piece[...] = value.astype(BF16)
        stages[3][p] = gather(p, 2, piece)
    for p in ENTRY:
        arrived(3, p)
        stages[4][p] = gather(p, 1, total.at[p, core, mine(p, 0), mine(p, 1)])
    for p in ENTRY:
        arrived(4, p)
        stages[5][p] = gather(p, 0, total.at[p, core, mine(p, 0)])
    last = []
    for p in ENTRY:
        arrived(5, p)
        last.append(remote(total.at[p, core], total.at[p, core], side_send.at[1, p], side_recv.at[1, p], other))
    for copy in last:
        copy.wait_recv()
    for group in stages:
        for copies in group:
            for copy in copies:
                copy.wait_send()
    for copy in swaps + first + last:
        copy.wait_send()


def back_step(*args):
    half = (3, 4, 4, 16, D)
    return pl.pallas_call(
        back_kernel,
        out_shape=(shape(3, 2, 4, 4, 16, D), shape(SIDE, N, D)),
        in_specs=[VM] * len(args),
        out_specs=(VM, VM),
        scratch_shapes=[
            pltpu.VMEM((SIDE, LOW, D), BF16),
            pltpu.VMEM((N, N), BF16),
            pltpu.VMEM((SIDE, N, D), BF16),
            pltpu.VMEM((SIDE, N, D), BF16),
            pltpu.VMEM((SIDE, N, D), BF16),
            pltpu.VMEM((SIDE, N, D), BF16),
            pltpu.VMEM((SIDE, D, N), BF16),
            pltpu.VMEM((SIDE, D, N), BF16),
            pltpu.VMEM((D, D), BF16),
            pltpu.VMEM((N, D), BF16),
            pltpu.VMEM((N, D), F32),
            pltpu.VMEM((3, 2, 4, 4, 16, D), F32),
            pltpu.VMEM(half, BF16),
            pltpu.VMEM(half, BF16),
            pltpu.VMEM(half, F32),
            pltpu.VMEM(half, BF16),
            pltpu.VMEM((3, 3, 4, 16, D), BF16),
            pltpu.VMEM((3, 4, 16, D), F32),
            pltpu.VMEM((3, 4, 16, D), BF16),
            pltpu.VMEM((3, 3, 16, D), BF16),
            pltpu.VMEM((3, 16, D), F32),
            pltpu.VMEM((3, 16, D), BF16),
            pltpu.VMEM((3, 3, 16, 128), BF16),
            pltpu.SemaphoreType.DMA((SIDE, 2)),
            pltpu.SemaphoreType.DMA((SIDE, 2)),
            pltpu.SemaphoreType.DMA((6, 3, 3)),
            pltpu.SemaphoreType.DMA((6, 3, 3)),
            pltpu.SemaphoreType.DMA((2, 3)),
            pltpu.SemaphoreType.DMA((2, 3)),
        ],
        compiler_params=pltpu.CompilerParams(
            collective_id=1, has_side_effects=True, vmem_limit_bytes=38 * 2**20
        ),
        cost_estimate=cost(12 * 2**30, 2**24),
    )(*args)


def local(
    features,
    tile_vals,
    tile_row,
    tile_col,
    send_next,
    send_prev,
    cluster,
    cotangent,
    self_weight,
    neighbour_weight,
    w_coarse,
):
    lab_row, lab_col, count, most, sums_c, low_c, got_prev, got_next = front(
        send_next, send_prev, cluster, features, cotangent
    )
    rec_c = partner(low_c)
    agg, hidden, slope, sums_h = node_step(
        tile_row, tile_col, lab_row, features, got_prev, got_next, tile_vals,
        self_weight, neighbour_weight,
    )
    far_h, far_c = lax.cond(
        most[0, 0] > LOW,
        lambda h, c: (partner(h[:, LOW:]), partner(c[:, LOW:])),
        lambda h, c: (jnp.zeros((SIDE, N - LOW, D), BF16),) * 2,
        sums_h,
        sums_c,
    )
    total, output = back_step(
        count, lab_col, sums_h, sums_c, rec_c, far_h, far_c, hidden, slope, agg, features, cotangent,
        w_coarse,
    )
    scale = 1.0 / math.sqrt(SIDE * lax.axis_size("batch") * N * lax.axis_size("dom"))
    totals = total.reshape(3, D, D).astype(F32)
    return output, totals[0] * scale, totals[1] * scale, totals[2] * scale


def solution(mesh):
    in_specs = (
        P("batch", "dom", None),
        P("dom", None, None),
        P("dom"),
        P("dom"),
        P("dom"),
        P("dom"),
        P("dom"),
        P("batch", "dom", None),
        P(),
        P(),
        P(),
    )
    out_specs = (P("batch", "dom", None), P(), P(), P())
    return jax.shard_map(local, mesh=mesh, in_specs=in_specs, out_specs=out_specs, check_vma=False)
```

```python
import math

import jax
import jax.numpy as jnp
from jax import lax
from jax.experimental import pallas as pl
from jax.experimental.pallas import tpu as pltpu
from jax.sharding import PartitionSpec as P

N = 1024
D = 512
BLK = 128
NB = 8
SIDE = 2
LOW = 576
F32 = jnp.float32
BF16 = jnp.bfloat16
VM = pl.BlockSpec(memory_space=pltpu.VMEM)
MESH = pl.DeviceIdType.MESH
SM = pl.BlockSpec(memory_space=pltpu.SMEM)
HB = pl.BlockSpec(memory_space=pltpu.HBM)


def partner(value):
    pairs = [(source, source ^ 1) for source in range(lax.axis_size("dom"))]
    return lax.ppermute(value, "dom", pairs)


def silu_pair(value):
    sig = jax.nn.sigmoid(value)
    return value * sig, sig * (1.0 + value * (1.0 - sig))


def dot(left, right):
    return jnp.dot(left, right, preferred_element_type=F32)


def dot_tn(left, right):
    return lax.dot_general(left, right, (((0,), (0,)), ((), ())), preferred_element_type=F32)


def dot_nt(left, right):
    return lax.dot_general(left, right, (((1,), (1,)), ((), ())), preferred_element_type=F32)


def shape(*dims, dtype=BF16):
    return jax.ShapeDtypeStruct(dims, dtype)


def cost(flops, size):
    return pl.CostEstimate(flops=flops, bytes_accessed=size, transcendentals=0)


class Place:
    def __init__(self):
        self.dom = lax.axis_index("dom")
        self.core = lax.axis_index("batch")
        self.at = (self.dom // 16, (self.dom // 4) % 4, self.dom % 4)

    def peer(self, axis, k):
        spot = (self.at[axis] + k) % 4
        return (self.dom + (spot - self.at[axis]) * (16, 4, 1)[axis], self.core), spot

    def across(self, first, second, k):
        spot, spot2 = (self.at[first] + k // 4) % 4, (self.at[second] + k % 4) % 4
        step = (spot - self.at[first]) * (16, 4, 1)[first] + (spot2 - self.at[second]) * (16, 4, 1)[second]
        return (self.dom + step, self.core), spot, spot2


def remote(src, dst, send, recv, device):
    copy = pltpu.make_async_remote_copy(
        src_ref=src, dst_ref=dst, send_sem=send, recv_sem=recv, device_id=device, device_id_type=MESH
    )
    copy.start()
    return copy


def greet(devices):
    barrier = pltpu.get_barrier_semaphore()
    for device in devices:
        pl.semaphore_signal(barrier, inc=1, device_id=device, device_id_type=MESH)
    return lambda: pl.semaphore_wait(barrier, len(devices))


def local_copy(src, dst, sem):
    copy = pltpu.make_async_copy(src, dst, sem)
    copy.start()
    return copy


def upright(row):
    return jnp.broadcast_to(row, (128, N)).T[:, :1]


def front_kernel(
    nexts_in, prevs_in, row_in, x_in, ct_in,
    lab_row, count, most, sums, low, got_prev, got_next,
    nexts, prevs, row_ref, x_ref, ct_ref, to_next, to_prev, table, held, rank, peak, peaks,
    load_sem, halo_send, halo_recv, peak_send, peak_recv,
):
    here = Place()
    nxt = ((here.dom + 1) % 64, here.core)
    prv = ((here.dom + 63) % 64, here.core)
    loads = [
        local_copy(src, dst, load_sem.at[i])
        for i, (src, dst) in enumerate(
            ((nexts_in, nexts), (prevs_in, prevs), (x_in, x_ref), (row_in, row_ref), (ct_in, ct_ref))
        )
    ]
    wait = greet([nxt, prv] + [here.peer(a, k)[0] for a in range(3) for k in (1, 2, 3)])
    for copy in loads[:3]:
        copy.wait()
    halo = []

    def take(s):
        for j in range(2):
            to_next[s, j] = x_ref[s, nexts[j]]
            to_prev[s, j] = x_ref[s, prevs[j]]

    def ship(s):
        halo.append(remote(to_next.at[s], got_prev.at[s], halo_send.at[0, s], halo_recv.at[0, s], nxt))
        halo.append(remote(to_prev.at[s], got_next.at[s], halo_send.at[1, s], halo_recv.at[1, s], prv))

    take(0)
    wait()
    ship(0)
    take(1)
    ship(1)
    loads[3].wait()
    row = row_ref[...]
    step = 128
    blocks = N // step

    def span(i):
        return pl.ds(pl.multiple_of(i * step, step), step)

    def downs(i):
        return lax.broadcasted_iota(jnp.int32, (step, N), 0) + i * step

    def wide(value):
        return jnp.broadcast_to(jnp.sum(value, axis=1, keepdims=True), (step, 128))

    def holding(i, carry):
        held[span(i), :] = wide(jnp.where(row == downs(i), 1.0, 0.0))
        return carry

    lax.fori_loop(0, blocks, holding, 0)
    held_row = held[...].T[:1]
    total = jnp.sum(jnp.where(held_row == 1.0, 1.0, 0.0), axis=1, keepdims=True)
    count[...] = jnp.broadcast_to(total, (8, 128)).astype(jnp.int32)
    peak[0] = jnp.broadcast_to(total, (8, 128))

    def spread(a):
        return [
            remote(peak.at[a], peaks.at[a, k - 1], peak_send.at[a, k - 1], peak_recv.at[a, k - 1], here.peer(a, k)[0])
            for k in (1, 2, 3)
        ]

    def settle(a, copies):
        for copy in copies:
            copy.wait()
        top = peak[a]
        for k in range(3):
            top = jnp.maximum(top, peaks[a, k])
        return top

    first = spread(0)
    both = jnp.where(held_row == 1.0, 1.0, jnp.where(held_row == 2.0, 2048.0, 0.0))

    def ranking(i, carry):
        across = lax.broadcasted_iota(jnp.int32, (step, N), 1)
        rank[span(i), :] = wide(jnp.where(across < downs(i), both, 0.0))
        return carry

    lax.fori_loop(0, blocks, ranking, 0)
    ranks = rank[:, :1].astype(jnp.int32)
    whole = total.astype(jnp.int32) + (ranks >> 11)
    rank[...] = jnp.broadcast_to(jnp.where(held[:, :1] == 1.0, ranks & 2047, whole), (N, 128)).astype(F32)

    def naming(i, carry):
        mine = jnp.where(row == downs(i), rank[span(i), :1], 0.0)
        return carry + jnp.sum(mine, axis=0, keepdims=True)

    label = lax.fori_loop(0, blocks, naming, jnp.zeros((1, N), F32)).astype(jnp.int32)
    lab_row[...] = label

    def one_hot(i, carry):
        table[span(i), :] = (label == downs(i)).astype(F32).astype(BF16)
        return carry

    lax.fori_loop(0, blocks, one_hot, 0)
    peak[1] = settle(0, first)
    second = spread(1)
    loads[4].wait()

    def pool(s):
        got = dot(table[...], ct_ref[s]).astype(BF16)
        sums[s] = got
        low[s] = got[:LOW]

    pool(0)
    peak[2] = settle(1, second)
    third = spread(2)
    pool(1)
    most[...] = settle(2, third).astype(jnp.int32)
    for copy in halo:
        copy.wait()

    @pl.when(here.dom == 0)
    def _():
        got_prev[...] = jnp.zeros_like(got_prev)

    @pl.when(here.dom == 63)
    def _():
        got_next[...] = jnp.zeros_like(got_next)


def front(send_next, send_prev, cluster, features, cotangent):
    halo = (SIDE, 2, BLK, D)
    return pl.pallas_call(
        front_kernel,
        out_shape=(
            shape(1, N, dtype=jnp.int32),
            shape(8, 128, dtype=jnp.int32),
            shape(8, 128, dtype=jnp.int32),
            shape(SIDE, N, D),
            shape(SIDE, LOW, D),
            shape(*halo),
            shape(*halo),
        ),
        in_specs=[HB] * 5,
        out_specs=(VM,) * 7,
        scratch_shapes=[
            pltpu.SMEM((2,), jnp.int32),
            pltpu.SMEM((2,), jnp.int32),
            pltpu.VMEM((1, N), jnp.int32),
            pltpu.VMEM((SIDE, NB, BLK, D), BF16),
            pltpu.VMEM((SIDE, N, D), BF16),
            pltpu.VMEM(halo, BF16),
            pltpu.VMEM(halo, BF16),
            pltpu.VMEM((N, N), BF16),
            pltpu.VMEM((N, 128), F32),
            pltpu.VMEM((N, 128), F32),
            pltpu.VMEM((3, 8, 128), F32),
            pltpu.VMEM((3, 3, 8, 128), F32),
            pltpu.SemaphoreType.DMA((5,)),
            pltpu.SemaphoreType.DMA((2, SIDE)),
            pltpu.SemaphoreType.DMA((2, SIDE)),
            pltpu.SemaphoreType.DMA((3, 3)),
            pltpu.SemaphoreType.DMA((3, 3)),
        ],
        compiler_params=pltpu.CompilerParams(
            collective_id=0, has_side_effects=True, vmem_limit_bytes=28 * 2**20
        ),
        cost_estimate=cost(4 * 2**30, 2**22),
    )(send_next, send_prev, cluster.reshape(1, N), features.reshape(SIDE, NB, BLK, D), cotangent)


def node_kernel(
    rows, cols, lab_row, x_ref, prev_ref, next_ref, tiles, w_self, w_neigh,
    agg, hidden, slope, sums, ext, acc, table,
):
    for s in range(SIDE):
        span = slice(s * D, (s + 1) * D)
        ext[0:NB, :, span] = x_ref[s].reshape(NB, BLK, D)
        ext[NB : NB + 2, :, span] = prev_ref[s]
        ext[NB + 2 : NB + 4, :, span] = next_ref[s]
    acc[...] = jnp.zeros_like(acc)

    def tile(t, carry):
        r = rows[t]
        acc[r] = acc[r] + dot(tiles[t], ext[cols[t]])
        return carry

    lax.fori_loop(0, tiles.shape[0], tile, 0)
    step = 256

    def block(i, carry):
        at = pl.ds(pl.multiple_of(i * step, step), step)
        down = lax.broadcasted_iota(jnp.int32, (step, N), 0) + i * step
        table[at, :] = (lab_row[...] == down).astype(F32).astype(BF16)
        for s in range(SIDE):
            span = slice(s * D, (s + 1) * D)
            got = acc[pl.ds(i * 2, 2), :, span].reshape(step, D).astype(BF16)
            agg[s, at, :] = got
            pre = dot(x_ref[s, at, :], w_self[...]) + dot(got, w_neigh[...])
            value, grad = silu_pair(pre)
            hidden[s, at, :] = value.astype(BF16)
            slope[s, at, :] = grad.astype(BF16)
        return carry

    lax.fori_loop(0, N // step, block, 0)
    for s in range(SIDE):
        sums[s] = dot(table[...], hidden[s]).astype(BF16)


def node_step(tile_row, tile_col, lab_row, features, got_prev, got_next, tiles, w_self, w_neigh):
    full = shape(SIDE, N, D)
    return pl.pallas_call(
        node_kernel,
        out_shape=(full,) * 4,
        in_specs=[SM, SM] + [VM] * 7,
        out_specs=(VM,) * 4,
        scratch_shapes=[
            pltpu.VMEM((NB + 4, BLK, SIDE * D), BF16),
            pltpu.VMEM((NB, BLK, SIDE * D), F32),
            pltpu.VMEM((N, N), BF16),
        ],
        compiler_params=pltpu.CompilerParams(vmem_limit_bytes=24 * 2**20),
        cost_estimate=cost(10 * 2**30, 2**23),
    )(tile_row, tile_col, lab_row, features, got_prev, got_next, tiles, w_self, w_neigh)


EARLY, MID, LAST = (640, 1024), (0, 384), (384, 640)
ORDERS = ((0, 1, 2), (1, 2, 0), (2, 0, 1))
ENTRY = (2, 0, 1)


def back_kernel(
    count, lab_row, w_coarse, sums_h_in, sums_c_in, rec_c_in, far_h_in, far_c_in, x_in, agg_in,
    ct_in, slope_in, hidden_in,
    total, out,
    sums_h, sums_c, rec_c, far_h, far_c, x_ref, agg, ct_ref, slope, hidden, load_sem,
    rec_h, flip, lifted, down, coarse, weighed, x_turn, a_turn, w_turn, grad_pre, part, grads,
    send0, recv0, acc, buf1, recv1, sum2, buf2, recv2,
    swap_send, swap_recv, send_sem, recv_sem, plane_send, plane_recv, side_send, side_recv,
):
    here = Place()
    core = here.core
    other = (here.dom, 1 - core)
    pair = (here.dom + 1 - 2 * (here.dom % 2), core)
    wait = greet([other, pair] + [here.peer(a, k)[0] for a in range(3) for k in (1, 2, 3)])
    wait()
    swaps, loads = [], []
    for s in range(SIDE):
        for i, (lo, hi) in enumerate((MID, (LAST[0], LOW))):
            rows = pl.ds(lo, hi - lo)
            swaps.append(
                remote(sums_h_in.at[s, rows], rec_h.at[s, rows], swap_send.at[s, i], swap_recv.at[s, i], pair)
            )

    for i, (src, dst) in enumerate(
        (
            (sums_h_in, sums_h), (sums_c_in, sums_c), (far_h_in, far_h), (far_c_in, far_c), (rec_c_in, rec_c),
            (x_in, x_ref), (agg_in, agg), (ct_in, ct_ref), (slope_in, slope), (hidden_in, hidden),
        )
    ):
        loads.append(local_copy(src, dst, load_sem.at[i]))
    label = upright(lab_row[...].astype(F32)).astype(jnp.int32)
    across = lax.broadcasted_iota(jnp.int32, (128, N), 1)
    for i in range(0, N, 128):
        flip[i : i + 128, :] = (label[i : i + 128] == across).astype(F32).astype(BF16)
    w_turn[...] = w_coarse[...].T
    for copy in loads[:5]:
        copy.wait()

    def level(s, span):
        lo, hi = span
        shared = lax.broadcasted_iota(jnp.int32, (hi - lo, 1), 0) + lo < count[0:1, 0:1]

        def joined(own, rec, far):
            if lo >= LOW:
                got = far[s, lo - LOW : hi - LOW]
            elif hi <= LOW:
                got = rec[s, lo:hi]
            else:
                got = jnp.concatenate([rec[s, lo:LOW], far[s, : hi - LOW]], axis=0)
            return own[s, lo:hi].astype(F32) + jnp.where(shared, got.astype(F32), 0.0)

        rows = (0.5 * joined(sums_h, rec_h, far_h)).astype(BF16)
        coarse[s, lo:hi] = rows
        value, grad = silu_pair(dot(rows, w_coarse[...]))
        lifted[s, lo:hi] = value.astype(BF16)
        grad_act = (joined(sums_c, rec_c, far_c) * grad).astype(BF16)
        down[s, lo:hi] = dot(grad_act, w_turn[...]).astype(BF16)
        weighed[s, lo:hi] = (grad_act.astype(F32) * jnp.where(shared, 0.5, 1.0)).astype(BF16)

    def looked(s, span):
        lo, hi = span
        return dot(flip[:, lo:hi], down[s, lo:hi])

    def product(s, span):
        lo, hi = span
        return dot_tn(coarse[s, lo:hi], weighed[s, lo:hi])

    def emit(s, lo, hi):
        out[s, lo:hi] = (hidden[s, lo:hi].astype(F32) + dot(flip[lo:hi, :], lifted[s])).astype(BF16)

    def store(p, value):
        grads[p] = value.reshape(2, 4, 4, 16, D)

    def load(p):
        return grads[p].reshape(D, D)

    for s in range(SIDE):
        level(s, EARLY)
    for copy in loads[5:]:
        copy.wait()
    for s in range(SIDE):
        x_turn[s] = x_ref[s].T
        a_turn[s] = agg[s].T

    swaps[0].wait_recv()
    level(0, MID)
    swaps[1].wait_recv()
    level(0, LAST)
    back = dot(flip[...], down[0])
    grad_pre[...] = ((ct_ref[0].astype(F32) + 0.5 * back) * slope[0].astype(F32)).astype(BF16)
    store(0, dot(x_turn[0], grad_pre[...]))
    store(1, dot(a_turn[0], grad_pre[...]))
    store(2, product(0, (0, N)) + product(1, EARLY))
    part[...] = looked(1, EARLY)
    emit(0, 0, N)

    swaps[2].wait_recv()
    level(1, MID)
    part[...] += looked(1, MID)
    store(2, load(2) + product(1, MID))
    swaps[3].wait_recv()
    level(1, LAST)
    first = [None] * 3

    def hand(p):
        send0[p] = grads[p, 1 - core].astype(BF16)
        first[p] = remote(send0.at[p], recv0.at[p], side_send.at[0, p], side_recv.at[0, p], other)

    store(2, load(2) + product(1, LAST))
    hand(2)
    back = part[...] + looked(1, LAST)
    grad_pre[...] = ((ct_ref[1].astype(F32) + 0.5 * back) * slope[1].astype(F32)).astype(BF16)
    store(0, load(0) + dot(x_turn[1], grad_pre[...]))
    hand(0)
    store(1, load(1) + dot(a_turn[1], grad_pre[...]))
    hand(1)

    def mine(p):
        return [here.at[axis] for axis in ORDERS[p]]

    def cols(spot):
        return pl.ds(pl.multiple_of(spot * 128, 128), 128)

    stages = [[None] * 3 for _ in range(4)]

    def arrived(stage, p):
        for copy in stages[stage][p]:
            copy.wait_recv()

    for p in ENTRY:
        first[p].wait_recv()
        value = grads[p, core] + recv0[p].astype(F32)
        acc[p] = value
        buf1[p] = value.astype(BF16)
        stages[0][p] = []
        for k in (1, 2, 3):
            device, spot = here.peer(ORDERS[p][0], k)
            stages[0][p].append(
                remote(buf1.at[p, spot], recv1.at[p, k - 1], send_sem.at[0, p, k - 1], recv_sem.at[0, p, k - 1], device)
            )
    emit(1, 0, 512)
    for p in ENTRY:
        arrived(0, p)
        value = acc[p, mine(p)[0]]
        for k in range(3):
            value = value + recv1[p, k].astype(F32)
        sum2[p] = value
        buf2[p] = value.astype(BF16)
    for p in ENTRY:
        stages[1][p] = []
        for k in range(1, 16):
            device, spot, spot2 = here.across(ORDERS[p][1], ORDERS[p][2], k)
            stages[1][p].append(
                remote(
                    buf2.at[p, spot, :, cols(spot2)], recv2.at[p, k - 1],
                    plane_send.at[0, p, k - 1], plane_recv.at[0, p, k - 1], device,
                )
            )
    emit(1, 512, 1024)
    for p in ENTRY:
        arrived(1, p)
        one, two, three = mine(p)
        value = sum2[p, two, :, cols(three)]
        for k in range(15):
            value = value + recv2[p, k].astype(F32)
        piece = total.at[p, core, one, two, :, cols(three)]
        piece[...] = value.astype(BF16)
        stages[2][p] = []
        for k in range(1, 16):
            device, _, _ = here.across(ORDERS[p][1], ORDERS[p][2], k)
            stages[2][p].append(
                remote(piece, piece, plane_send.at[1, p, k - 1], plane_recv.at[1, p, k - 1], device)
            )
    for p in ENTRY:
        arrived(2, p)
        piece = total.at[p, core, mine(p)[0]]
        stages[3][p] = []
        for k in (1, 2, 3):
            device, _ = here.peer(ORDERS[p][0], k)
            stages[3][p].append(
                remote(piece, piece, send_sem.at[1, p, k - 1], recv_sem.at[1, p, k - 1], device)
            )
    last = []
    for p in ENTRY:
        arrived(3, p)
        last.append(remote(total.at[p, core], total.at[p, core], side_send.at[1, p], side_recv.at[1, p], other))
    for copy in last:
        copy.wait_recv()
    for group in stages:
        for copies in group:
            for copy in copies:
                copy.wait_send()
    for copy in swaps + first + last:
        copy.wait_send()


def back_step(*args):
    half = (3, 4, 4, 16, D)
    return pl.pallas_call(
        back_kernel,
        out_shape=(shape(3, 2, 4, 4, 16, D), shape(SIDE, N, D)),
        in_specs=[VM] * 3 + [HB] * (len(args) - 3),
        out_specs=(VM, VM),
        scratch_shapes=[
            pltpu.VMEM((SIDE, N, D), BF16),
            pltpu.VMEM((SIDE, N, D), BF16),
            pltpu.VMEM((SIDE, LOW, D), BF16),
            pltpu.VMEM((SIDE, N - LOW, D), BF16),
            pltpu.VMEM((SIDE, N - LOW, D), BF16),
            pltpu.VMEM((SIDE, N, D), BF16),
            pltpu.VMEM((SIDE, N, D), BF16),
            pltpu.VMEM((SIDE, N, D), BF16),
            pltpu.VMEM((SIDE, N, D), BF16),
            pltpu.VMEM((SIDE, N, D), BF16),
            pltpu.SemaphoreType.DMA((10,)),
            pltpu.VMEM((SIDE, LOW, D), BF16),
            pltpu.VMEM((N, N), BF16),
            pltpu.VMEM((SIDE, N, D), BF16),
            pltpu.VMEM((SIDE, N, D), BF16),
            pltpu.VMEM((SIDE, N, D), BF16),
            pltpu.VMEM((SIDE, N, D), BF16),
            pltpu.VMEM((SIDE, D, N), BF16),
            pltpu.VMEM((SIDE, D, N), BF16),
            pltpu.VMEM((D, D), BF16),
            pltpu.VMEM((N, D), BF16),
            pltpu.VMEM((N, D), F32),
            pltpu.VMEM((3, 2, 4, 4, 16, D), F32),
            pltpu.VMEM(half, BF16),
            pltpu.VMEM(half, BF16),
            pltpu.VMEM(half, F32),
            pltpu.VMEM(half, BF16),
            pltpu.VMEM((3, 3, 4, 16, D), BF16),
            pltpu.VMEM((3, 4, 16, D), F32),
            pltpu.VMEM((3, 4, 16, D), BF16),
            pltpu.VMEM((3, 15, 16, 128), BF16),
            pltpu.SemaphoreType.DMA((SIDE, 2)),
            pltpu.SemaphoreType.DMA((SIDE, 2)),
            pltpu.SemaphoreType.DMA((2, 3, 3)),
            pltpu.SemaphoreType.DMA((2, 3, 3)),
            pltpu.SemaphoreType.DMA((2, 3, 15)),
            pltpu.SemaphoreType.DMA((2, 3, 15)),
            pltpu.SemaphoreType.DMA((2, 3)),
            pltpu.SemaphoreType.DMA((2, 3)),
        ],
        compiler_params=pltpu.CompilerParams(
            collective_id=1, has_side_effects=True, vmem_limit_bytes=56 * 2**20
        ),
        cost_estimate=cost(12 * 2**30, 2**24),
    )(*args)


def local(
    features,
    tile_vals,
    tile_row,
    tile_col,
    send_next,
    send_prev,
    cluster,
    cotangent,
    self_weight,
    neighbour_weight,
    w_coarse,
):
    lab_row, count, most, sums_c, low_c, got_prev, got_next = front(
        send_next, send_prev, cluster, features, cotangent
    )
    rec_c = partner(low_c)
    agg, hidden, slope, sums_h = node_step(
        tile_row, tile_col, lab_row, features, got_prev, got_next, tile_vals,
        self_weight, neighbour_weight,
    )
    far_h, far_c = lax.cond(
        most[0, 0] > LOW,
        lambda h, c: (partner(h[:, LOW:]), partner(c[:, LOW:])),
        lambda h, c: (jnp.zeros((SIDE, N - LOW, D), BF16),) * 2,
        sums_h,
        sums_c,
    )
    total, output = back_step(
        count, lab_row, w_coarse, sums_h, sums_c, rec_c, far_h, far_c, features, agg, cotangent, slope,
        hidden,
    )
    scale = 1.0 / math.sqrt(SIDE * lax.axis_size("batch") * N * lax.axis_size("dom"))
    return (output,) + tuple(total[p].reshape(D, D).astype(F32) * scale for p in range(3))


def solution(mesh):
    in_specs = (
        P("batch", "dom", None),
        P("dom", None, None),
        P("dom"),
        P("dom"),
        P("dom"),
        P("dom"),
        P("dom"),
        P("batch", "dom", None),
        P(),
        P(),
        P(),
    )
    out_specs = (P("batch", "dom", None), P(), P(), P())
    return jax.shard_map(local, mesh=mesh, in_specs=in_specs, out_specs=out_specs, check_vma=False)
```

```python
import functools
import math

import jax
import jax.numpy as jnp
from jax import lax
from jax.experimental import pallas as pl
from jax.experimental.pallas import tpu as pltpu
from jax.sharding import PartitionSpec as P

N = 1024
D = 512
BLK = 128
NB = 8
SIDE = 2
LOW = 576
HEAD = 160
F32 = jnp.float32
BF16 = jnp.bfloat16
VM = pl.BlockSpec(memory_space=pltpu.VMEM)
MESH = pl.DeviceIdType.MESH
SM = pl.BlockSpec(memory_space=pltpu.SMEM)
HB = pl.BlockSpec(memory_space=pl.ANY)


def partner(value):
    pairs = [(source, source ^ 1) for source in range(lax.axis_size("dom"))]
    return lax.ppermute(value, "dom", pairs)


def silu_pair(value):
    sig = jax.nn.sigmoid(value)
    return value * sig, sig * (1.0 + value * (1.0 - sig))


def dot(left, right):
    return jnp.dot(left, right, preferred_element_type=F32)


def dot_tn(left, right):
    return lax.dot_general(left, right, (((0,), (0,)), ((), ())), preferred_element_type=F32)


def dot_nt(left, right):
    return lax.dot_general(left, right, (((1,), (1,)), ((), ())), preferred_element_type=F32)


def shape(*dims, dtype=BF16):
    return jax.ShapeDtypeStruct(dims, dtype)


def in_hbm(value):
    return pltpu.with_memory_space_constraint(value, pltpu.HBM)


def cost(flops, size):
    return pl.CostEstimate(flops=flops, bytes_accessed=size, transcendentals=0)


class Place:
    def __init__(self):
        self.dom = lax.axis_index("dom")
        self.core = lax.axis_index("batch")
        self.at = (self.dom // 16, (self.dom // 4) % 4, self.dom % 4)

    def peer(self, axis, k):
        spot = (self.at[axis] + k) % 4
        return (self.dom + (spot - self.at[axis]) * (16, 4, 1)[axis], self.core), spot

    def across(self, first, second, k):
        spot, spot2 = (self.at[first] + k // 4) % 4, (self.at[second] + k % 4) % 4
        step = (spot - self.at[first]) * (16, 4, 1)[first] + (spot2 - self.at[second]) * (16, 4, 1)[second]
        return (self.dom + step, self.core), spot, spot2


def remote(src, dst, send, recv, device):
    copy = pltpu.make_async_remote_copy(
        src_ref=src, dst_ref=dst, send_sem=send, recv_sem=recv, device_id=device, device_id_type=MESH
    )
    copy.start()
    return copy


def greet(devices):
    barrier = pltpu.get_barrier_semaphore()
    for device in devices:
        pl.semaphore_signal(barrier, inc=1, device_id=device, device_id_type=MESH)
    return lambda: pl.semaphore_wait(barrier, len(devices))


def local_copy(src, dst, sem):
    copy = pltpu.make_async_copy(src, dst, sem)
    copy.start()
    return copy


def upright(row):
    return jnp.broadcast_to(row, (128, N)).T[:, :1]


def front_kernel(
    nexts_in, prevs_in, row_in, x_in, ct_in,
    lab_row, count, most, sums, low, head, got_prev, got_next,
    nexts, prevs, row_ref, x_ref, ct_ref, to_next, to_prev, table, held, rank, peak, peaks,
    load_sem, halo_send, halo_recv, peak_send, peak_recv, head_send, head_recv,
):
    here = Place()
    pair = (here.dom + 1 - 2 * (here.dom % 2), here.core)
    nxt = ((here.dom + 1) % 64, here.core)
    prv = ((here.dom + 63) % 64, here.core)
    loads = [
        local_copy(src, dst, load_sem.at[i])
        for i, (src, dst) in enumerate(
            ((nexts_in, nexts), (prevs_in, prevs), (x_in, x_ref), (row_in, row_ref), (ct_in, ct_ref))
        )
    ]
    wait = greet([nxt, prv] + [here.peer(a, k)[0] for a in range(3) for k in (1, 2, 3)])
    for copy in loads[:3]:
        copy.wait()
    halo = []

    def take(s):
        for j in range(2):
            to_next[s, j] = x_ref[s, nexts[j]]
            to_prev[s, j] = x_ref[s, prevs[j]]

    def ship(s):
        halo.append(remote(to_next.at[s], got_prev.at[s], halo_send.at[0, s], halo_recv.at[0, s], nxt))
        halo.append(remote(to_prev.at[s], got_next.at[s], halo_send.at[1, s], halo_recv.at[1, s], prv))

    take(0)
    wait()
    ship(0)
    take(1)
    ship(1)
    loads[3].wait()
    row = row_ref[...]
    step = 128
    blocks = N // step

    def span(i):
        return pl.ds(pl.multiple_of(i * step, step), step)

    def downs(i):
        return lax.broadcasted_iota(jnp.int32, (step, N), 0) + i * step

    def wide(value):
        return jnp.broadcast_to(jnp.sum(value, axis=1, keepdims=True), (step, 128))

    def holding(i, carry):
        held[span(i), :] = wide(jnp.where(row == downs(i), 1.0, 0.0))
        return carry

    lax.fori_loop(0, blocks, holding, 0)
    held_row = held[...].T[:1]
    total = jnp.sum(jnp.where(held_row == 1.0, 1.0, 0.0), axis=1, keepdims=True)
    count[...] = jnp.broadcast_to(total, (8, 128)).astype(jnp.int32)
    peak[0] = jnp.broadcast_to(total, (8, 128))

    def spread(a):
        return [
            remote(peak.at[a], peaks.at[a, k - 1], peak_send.at[a, k - 1], peak_recv.at[a, k - 1], here.peer(a, k)[0])
            for k in (1, 2, 3)
        ]

    def settle(a, copies):
        for copy in copies:
            copy.wait()
        top = peak[a]
        for k in range(3):
            top = jnp.maximum(top, peaks[a, k])
        return top

    first = spread(0)
    both = jnp.where(held_row == 1.0, 1.0, jnp.where(held_row == 2.0, 2048.0, 0.0))

    def ranking(i, carry):
        across = lax.broadcasted_iota(jnp.int32, (step, N), 1)
        rank[span(i), :] = wide(jnp.where(across < downs(i), both, 0.0))
        return carry

    lax.fori_loop(0, blocks, ranking, 0)
    ranks = rank[:, :1].astype(jnp.int32)
    whole = total.astype(jnp.int32) + (ranks >> 11)
    rank[...] = jnp.broadcast_to(jnp.where(held[:, :1] == 1.0, ranks & 2047, whole), (N, 128)).astype(F32)

    def naming(i, carry):
        mine = jnp.where(row == downs(i), rank[span(i), :1], 0.0)
        return carry + jnp.sum(mine, axis=0, keepdims=True)

    label = lax.fori_loop(0, blocks, naming, jnp.zeros((1, N), F32)).astype(jnp.int32)
    lab_row[...] = label

    def one_hot(i, carry):
        table[span(i), :] = (label == downs(i)).astype(F32).astype(BF16)
        return carry

    lax.fori_loop(0, blocks, one_hot, 0)
    peak[1] = settle(0, first)
    second = spread(1)
    loads[4].wait()

    def pool(s):
        got = dot(table[...], ct_ref[s]).astype(BF16)
        sums[s] = got
        low[s] = got[HEAD:LOW]
        halo.append(remote(sums.at[s, pl.ds(0, HEAD)], head.at[s], head_send.at[s], head_recv.at[s], pair))

    pool(0)
    peak[2] = settle(1, second)
    third = spread(2)
    pool(1)
    most[...] = settle(2, third).astype(jnp.int32)
    for copy in halo:
        copy.wait()

    @pl.when(here.dom == 0)
    def _():
        got_prev[...] = jnp.zeros_like(got_prev)

    @pl.when(here.dom == 63)
    def _():
        got_next[...] = jnp.zeros_like(got_next)


def front(send_next, send_prev, cluster, features, cotangent):
    halo = (SIDE, 2, BLK, D)
    return pl.pallas_call(
        front_kernel,
        out_shape=(
            shape(1, N, dtype=jnp.int32),
            shape(8, 128, dtype=jnp.int32),
            shape(8, 128, dtype=jnp.int32),
            shape(SIDE, N, D),
            shape(SIDE, LOW - HEAD, D),
            shape(SIDE, HEAD, D),
            shape(*halo),
            shape(*halo),
        ),
        in_specs=[HB] * 5,
        out_specs=(VM,) * 8,
        scratch_shapes=[
            pltpu.SMEM((2,), jnp.int32),
            pltpu.SMEM((2,), jnp.int32),
            pltpu.VMEM((1, N), jnp.int32),
            pltpu.VMEM((SIDE, NB, BLK, D), BF16),
            pltpu.VMEM((SIDE, N, D), BF16),
            pltpu.VMEM(halo, BF16),
            pltpu.VMEM(halo, BF16),
            pltpu.VMEM((N, N), BF16),
            pltpu.VMEM((N, 128), F32),
            pltpu.VMEM((N, 128), F32),
            pltpu.VMEM((3, 8, 128), F32),
            pltpu.VMEM((3, 3, 8, 128), F32),
            pltpu.SemaphoreType.DMA((5,)),
            pltpu.SemaphoreType.DMA((2, SIDE)),
            pltpu.SemaphoreType.DMA((2, SIDE)),
            pltpu.SemaphoreType.DMA((3, 3)),
            pltpu.SemaphoreType.DMA((3, 3)),
            pltpu.SemaphoreType.DMA((SIDE,)),
            pltpu.SemaphoreType.DMA((SIDE,)),
        ],
        compiler_params=pltpu.CompilerParams(
            collective_id=0, has_side_effects=True, vmem_limit_bytes=24 * 2**20
        ),
        cost_estimate=cost(4 * 2**30, 2**22),
    )(
        in_hbm(send_next), in_hbm(send_prev), in_hbm(cluster.reshape(1, N)),
        in_hbm(features.reshape(SIDE, NB, BLK, D)), in_hbm(cotangent),
    )


def node_kernel(
    rows, cols, lab_row, x_ref, prev_ref, next_ref, tiles, w_self, w_neigh,
    agg_out, hidden_out, slope_out, sums_out, agg, hidden, slope, sums, ext, acc, table, sem,
):
    for s in range(SIDE):
        span = slice(s * D, (s + 1) * D)
        ext[0:NB, :, span] = x_ref[s].reshape(NB, BLK, D)
        ext[NB : NB + 2, :, span] = prev_ref[s]
        ext[NB + 2 : NB + 4, :, span] = next_ref[s]
    acc[...] = jnp.zeros_like(acc)

    def tile(t, carry):
        r = rows[t]
        acc[r] = acc[r] + dot(tiles[t], ext[cols[t]])
        return carry

    lax.fori_loop(0, tiles.shape[0], tile, 0)
    step = 256

    def block(i, carry):
        at = pl.ds(pl.multiple_of(i * step, step), step)
        down = lax.broadcasted_iota(jnp.int32, (step, N), 0) + i * step
        table[at, :] = (lab_row[...] == down).astype(F32).astype(BF16)
        for s in range(SIDE):
            span = slice(s * D, (s + 1) * D)
            got = acc[pl.ds(i * 2, 2), :, span].reshape(step, D).astype(BF16)
            agg[s, at, :] = got
            pre = dot(x_ref[s, at, :], w_self[...]) + dot(got, w_neigh[...])
            value, grad = silu_pair(pre)
            hidden[s, at, :] = value.astype(BF16)
            slope[s, at, :] = grad.astype(BF16)
        return carry

    lax.fori_loop(0, N // step, block, 0)
    copies = [
        local_copy(src, dst, sem.at[i])
        for i, (src, dst) in enumerate(((agg, agg_out), (hidden, hidden_out), (slope, slope_out)))
    ]
    for s in range(SIDE):
        sums[s] = dot(table[...], hidden[s]).astype(BF16)
        copies.append(local_copy(sums.at[s], sums_out.at[s], sem.at[3 + s]))
    for copy in copies:
        copy.wait()


def node_step(tile_row, tile_col, lab_row, features, got_prev, got_next, tiles, w_self, w_neigh):
    full = pltpu.HBM((SIDE, N, D), BF16)
    return pl.pallas_call(
        node_kernel,
        out_shape=(full,) * 4,
        in_specs=[SM, SM] + [VM] * 7,
        out_specs=(HB,) * 4,
        scratch_shapes=[
            pltpu.VMEM((SIDE, N, D), BF16),
            pltpu.VMEM((SIDE, N, D), BF16),
            pltpu.VMEM((SIDE, N, D), BF16),
            pltpu.VMEM((SIDE, N, D), BF16),
            pltpu.VMEM((NB + 4, BLK, SIDE * D), BF16),
            pltpu.VMEM((NB, BLK, SIDE * D), F32),
            pltpu.VMEM((N, N), BF16),
            pltpu.SemaphoreType.DMA((5,)),
        ],
        compiler_params=pltpu.CompilerParams(vmem_limit_bytes=34 * 2**20),
        cost_estimate=cost(10 * 2**30, 2**23),
    )(tile_row, tile_col, lab_row, features, got_prev, got_next, tiles, w_self, w_neigh)


EARLY = (640, 1024)
CHUNKS = (((0, 384), (384, 640)), ((0, 256), (256, 512), (512, 640)))
ORDERS = ((0, 1, 2), (1, 2, 0), (2, 0, 1))
ENTRY = (2, 0, 1)


def back_kernel(
    count, lab_row, w_coarse, sums_h_in, sums_c_in, head_in, rec_c_in, far_h_in, far_c_in, x_in, agg_in,
    ct_in, slope_in, hidden_in,
    total, out,
    sums_h, sums_c, rec_c, far_h, far_c, x_ref, agg, ct_ref, slope, hidden, load_sem,
    rec_h, flip, lifted, down, coarse, weighed, x_turn, a_turn, w_turn, grad_pre, part, grads,
    send0, recv0, acc, buf1, recv1, sum2, buf2, recv2,
    swap_send, swap_recv, send_sem, recv_sem, plane_send, plane_recv, side_send, side_recv,
):
    here = Place()
    core = here.core
    other = (here.dom, 1 - core)
    pair = (here.dom + 1 - 2 * (here.dom % 2), core)
    wait = greet([other, pair] + [here.peer(a, k)[0] for a in range(3) for k in (1, 2, 3)])
    wait()
    swaps, loads = [], []
    for s in range(SIDE):
        for i, (lo, hi) in enumerate(CHUNKS[s]):
            rows = pl.ds(lo, min(hi, LOW) - lo)
            swaps.append(
                remote(sums_h_in.at[s, rows], rec_h.at[s, rows], swap_send.at[s, i], swap_recv.at[s, i], pair)
            )

    for i, (src, dst) in enumerate(
        (
            (sums_h_in, sums_h), (sums_c_in, sums_c), (far_h_in, far_h), (far_c_in, far_c),
            (head_in, rec_c.at[:, pl.ds(0, HEAD)]), (rec_c_in, rec_c.at[:, pl.ds(HEAD, LOW - HEAD)]),
            (x_in, x_ref), (agg_in, agg), (ct_in, ct_ref), (slope_in, slope), (hidden_in, hidden),
        )
    ):
        loads.append(local_copy(src, dst, load_sem.at[i]))
    label = upright(lab_row[...].astype(F32)).astype(jnp.int32)
    across = lax.broadcasted_iota(jnp.int32, (128, N), 1)
    for i in range(0, N, 128):
        flip[i : i + 128, :] = (label[i : i + 128] == across).astype(F32).astype(BF16)
    w_turn[...] = w_coarse[...].T
    for copy in loads[:6]:
        copy.wait()

    def level(s, span):
        lo, hi = span
        shared = lax.broadcasted_iota(jnp.int32, (hi - lo, 1), 0) + lo < count[0:1, 0:1]

        def joined(own, rec, far):
            if lo >= LOW:
                got = far[s, lo - LOW : hi - LOW]
            elif hi <= LOW:
                got = rec[s, lo:hi]
            else:
                got = jnp.concatenate([rec[s, lo:LOW], far[s, : hi - LOW]], axis=0)
            return own[s, lo:hi].astype(F32) + jnp.where(shared, got.astype(F32), 0.0)

        rows = (0.5 * joined(sums_h, rec_h, far_h)).astype(BF16)
        coarse[s, lo:hi] = rows
        value, grad = silu_pair(dot(rows, w_coarse[...]))
        lifted[s, lo:hi] = value.astype(BF16)
        grad_act = (joined(sums_c, rec_c, far_c) * grad).astype(BF16)
        down[s, lo:hi] = dot(grad_act, w_turn[...]).astype(BF16)
        weighed[s, lo:hi] = (grad_act.astype(F32) * jnp.where(shared, 0.5, 1.0)).astype(BF16)

    def looked(s, span):
        lo, hi = span
        return dot(flip[:, lo:hi], down[s, lo:hi])

    def product(s, span):
        lo, hi = span
        return dot_tn(coarse[s, lo:hi], weighed[s, lo:hi])

    def emit(s, lo, hi):
        out[s, lo:hi] = (hidden[s, lo:hi].astype(F32) + dot(flip[lo:hi, :], lifted[s])).astype(BF16)

    def store(p, value):
        grads[p] = value.reshape(2, 4, 4, 16, D)

    def load(p):
        return grads[p].reshape(D, D)

    for s in range(SIDE):
        level(s, EARLY)
    for copy in loads[6:]:
        copy.wait()
    for s in range(SIDE):
        x_turn[s] = x_ref[s].T
        a_turn[s] = agg[s].T

    for i, span in enumerate(CHUNKS[0]):
        swaps[i].wait_recv()
        level(0, span)
    back = dot(flip[...], down[0])
    grad_pre[...] = ((ct_ref[0].astype(F32) + 0.5 * back) * slope[0].astype(F32)).astype(BF16)
    store(0, dot(x_turn[0], grad_pre[...]))
    store(1, dot(a_turn[0], grad_pre[...]))
    store(2, product(0, (0, N)) + product(1, EARLY))
    part[...] = looked(1, EARLY)
    emit(0, 0, N)
    for i, span in enumerate(CHUNKS[1][:-1]):
        swaps[2 + i].wait_recv()
        level(1, span)
        part[...] += looked(1, span)
        store(2, load(2) + product(1, span))
    LAST = CHUNKS[1][-1]
    swaps[4].wait_recv()
    level(1, LAST)
    first = [None] * 3

    def hand(p):
        send0[p] = grads[p, 1 - core].astype(BF16)
        first[p] = remote(send0.at[p], recv0.at[p], side_send.at[0, p], side_recv.at[0, p], other)

    store(2, load(2) + product(1, LAST))
    hand(2)
    back = part[...] + looked(1, LAST)
    grad_pre[...] = ((ct_ref[1].astype(F32) + 0.5 * back) * slope[1].astype(F32)).astype(BF16)
    store(0, load(0) + dot(x_turn[1], grad_pre[...]))
    hand(0)
    store(1, load(1) + dot(a_turn[1], grad_pre[...]))
    hand(1)

    def mine(p):
        return [here.at[axis] for axis in ORDERS[p]]

    def cols(spot):
        return pl.ds(pl.multiple_of(spot * 128, 128), 128)

    stages = [[None] * 3 for _ in range(4)]

    def arrived(stage, p):
        for copy in stages[stage][p]:
            copy.wait_recv()

    for p in ENTRY:
        first[p].wait_recv()
        value = grads[p, core] + recv0[p].astype(F32)
        acc[p] = value
        buf1[p] = value.astype(BF16)
        stages[0][p] = []
        for k in (1, 2, 3):
            device, spot = here.peer(ORDERS[p][0], k)
            stages[0][p].append(
                remote(buf1.at[p, spot], recv1.at[p, k - 1], send_sem.at[0, p, k - 1], recv_sem.at[0, p, k - 1], device)
            )
    emit(1, 0, 512)
    for p in ENTRY:
        arrived(0, p)
        value = acc[p, mine(p)[0]]
        for k in range(3):
            value = value + recv1[p, k].astype(F32)
        sum2[p] = value
        buf2[p] = value.astype(BF16)
    for p in ENTRY:
        stages[1][p] = []
        for k in range(1, 16):
            device, spot, spot2 = here.across(ORDERS[p][1], ORDERS[p][2], k)
            stages[1][p].append(
                remote(
                    buf2.at[p, spot, :, cols(spot2)], recv2.at[p, k - 1],
                    plane_send.at[0, p, k - 1], plane_recv.at[0, p, k - 1], device,
                )
            )
    emit(1, 512, 1024)
    for p in ENTRY:
        arrived(1, p)
        one, two, three = mine(p)
        value = sum2[p, two, :, cols(three)]
        for k in range(15):
            value = value + recv2[p, k].astype(F32)
        piece = total.at[p, core, one, two, :, cols(three)]
        piece[...] = value.astype(BF16)
        stages[2][p] = []
        for k in range(1, 16):
            device, _, _ = here.across(ORDERS[p][1], ORDERS[p][2], k)
            stages[2][p].append(
                remote(piece, piece, plane_send.at[1, p, k - 1], plane_recv.at[1, p, k - 1], device)
            )
    for p in ENTRY:
        arrived(2, p)
        piece = total.at[p, core, mine(p)[0]]
        stages[3][p] = []
        for k in (1, 2, 3):
            device, _ = here.peer(ORDERS[p][0], k)
            stages[3][p].append(
                remote(piece, piece, send_sem.at[1, p, k - 1], recv_sem.at[1, p, k - 1], device)
            )
    last = []
    for p in ENTRY:
        arrived(3, p)
        last.append(remote(total.at[p, core], total.at[p, core], side_send.at[1, p], side_recv.at[1, p], other))
    for copy in last:
        copy.wait_recv()
    for group in stages:
        for copies in group:
            for copy in copies:
                copy.wait_send()
    for copy in swaps + first + last:
        copy.wait_send()


def back_step(*args):
    half = (3, 4, 4, 16, D)
    return pl.pallas_call(
        back_kernel,
        out_shape=(shape(3, 2, 4, 4, 16, D), shape(SIDE, N, D)),
        in_specs=[VM] * 3 + [HB] * (len(args) - 3),
        out_specs=(VM, VM),
        scratch_shapes=[
            pltpu.VMEM((SIDE, N, D), BF16),
            pltpu.VMEM((SIDE, N, D), BF16),
            pltpu.VMEM((SIDE, LOW, D), BF16),
            pltpu.VMEM((SIDE, N - LOW, D), BF16),
            pltpu.VMEM((SIDE, N - LOW, D), BF16),
            pltpu.VMEM((SIDE, N, D), BF16),
            pltpu.VMEM((SIDE, N, D), BF16),
            pltpu.VMEM((SIDE, N, D), BF16),
            pltpu.VMEM((SIDE, N, D), BF16),
            pltpu.VMEM((SIDE, N, D), BF16),
            pltpu.SemaphoreType.DMA((11,)),
            pltpu.VMEM((SIDE, LOW, D), BF16),
            pltpu.VMEM((N, N), BF16),
            pltpu.VMEM((SIDE, N, D), BF16),
            pltpu.VMEM((SIDE, N, D), BF16),
            pltpu.VMEM((SIDE, N, D), BF16),
            pltpu.VMEM((SIDE, N, D), BF16),
            pltpu.VMEM((SIDE, D, N), BF16),
            pltpu.VMEM((SIDE, D, N), BF16),
            pltpu.VMEM((D, D), BF16),
            pltpu.VMEM((N, D), BF16),
            pltpu.VMEM((N, D), F32),
            pltpu.VMEM((3, 2, 4, 4, 16, D), F32),
            pltpu.VMEM(half, BF16),
            pltpu.VMEM(half, BF16),
            pltpu.VMEM(half, F32),
            pltpu.VMEM(half, BF16),
            pltpu.VMEM((3, 3, 4, 16, D), BF16),
            pltpu.VMEM((3, 4, 16, D), F32),
            pltpu.VMEM((3, 4, 16, D), BF16),
            pltpu.VMEM((3, 15, 16, 128), BF16),
            pltpu.SemaphoreType.DMA((SIDE, 3)),
            pltpu.SemaphoreType.DMA((SIDE, 3)),
            pltpu.SemaphoreType.DMA((2, 3, 3)),
            pltpu.SemaphoreType.DMA((2, 3, 3)),
            pltpu.SemaphoreType.DMA((2, 3, 15)),
            pltpu.SemaphoreType.DMA((2, 3, 15)),
            pltpu.SemaphoreType.DMA((2, 3)),
            pltpu.SemaphoreType.DMA((2, 3)),
        ],
        compiler_params=pltpu.CompilerParams(
            collective_id=1, has_side_effects=True, vmem_limit_bytes=46 * 2**20
        ),
        cost_estimate=cost(12 * 2**30, 2**24),
    )(*args[:3], *(in_hbm(arg) for arg in args[3:]))


def close_kernel(scale, total, out_in, out, g0, g1, g2, wide, sem):
    copies = [local_copy(out_in.at[s], out.at[s], sem.at[3 + s]) for s in range(SIDE)]
    for p, g in enumerate((g0, g1, g2)):
        wide[p] = total[p].astype(F32) * scale
        copies.append(local_copy(wide.at[p], g, sem.at[p]))
    for copy in copies:
        copy.wait()


def close(scale, total, out):
    return pl.pallas_call(
        functools.partial(close_kernel, scale),
        out_shape=(shape(SIDE, N, D),) + (shape(D, D, dtype=F32),) * 3,
        in_specs=[VM, VM],
        out_specs=(HB,) * 4,
        scratch_shapes=[pltpu.VMEM((3, D, D), F32), pltpu.SemaphoreType.DMA((5,))],
        compiler_params=pltpu.CompilerParams(vmem_limit_bytes=8 * 2**20),
    )(total, out)


def local(
    features,
    tile_vals,
    tile_row,
    tile_col,
    send_next,
    send_prev,
    cluster,
    cotangent,
    self_weight,
    neighbour_weight,
    w_coarse,
):
    lab_row, count, most, sums_c, low_c, head_c, got_prev, got_next = front(
        send_next, send_prev, cluster, features, cotangent
    )
    rec_c = partner(low_c)
    agg, hidden, slope, sums_h = node_step(
        tile_row, tile_col, lab_row, features, got_prev, got_next, tile_vals,
        self_weight, neighbour_weight,
    )
    far_h, far_c = lax.cond(
        most[0, 0] > LOW,
        lambda h, c: (partner(h[:, LOW:]), partner(c[:, LOW:])),
        lambda h, c: (jnp.zeros((SIDE, N - LOW, D), BF16),) * 2,
        sums_h,
        sums_c,
    )
    total, output = back_step(
        count, lab_row, w_coarse, sums_h, sums_c, head_c, rec_c, far_h, far_c, features, agg, cotangent, slope,
        hidden,
    )
    scale = 1.0 / math.sqrt(SIDE * lax.axis_size("batch") * N * lax.axis_size("dom"))
    return close(scale, total.reshape(3, D, D), output)


def solution(mesh):
    in_specs = (
        P("batch", "dom", None),
        P("dom", None, None),
        P("dom"),
        P("dom"),
        P("dom"),
        P("dom"),
        P("dom"),
        P("batch", "dom", None),
        P(),
        P(),
        P(),
    )
    out_specs = (P("batch", "dom", None), P(), P(), P())
    return jax.shard_map(local, mesh=mesh, in_specs=in_specs, out_specs=out_specs, check_vma=False)
```

```python
import functools
import math

import jax
import jax.numpy as jnp
from jax import lax
from jax.experimental import pallas as pl
from jax.experimental.pallas import tpu as pltpu
from jax.sharding import PartitionSpec as P

N = 1024
D = 512
BLK = 128
NB = 8
SIDE = 2
LOW = 576
HEAD = 176
F32 = jnp.float32
BF16 = jnp.bfloat16
VM = pl.BlockSpec(memory_space=pltpu.VMEM)
MESH = pl.DeviceIdType.MESH
SM = pl.BlockSpec(memory_space=pltpu.SMEM)
HB = pl.BlockSpec(memory_space=pl.ANY)


def partner(value):
    pairs = [(source, source ^ 1) for source in range(lax.axis_size("dom"))]
    return lax.ppermute(value, "dom", pairs)


def silu_pair(value):
    sig = jax.nn.sigmoid(value)
    return value * sig, sig * (1.0 + value * (1.0 - sig))


def dot(left, right):
    return jnp.dot(left, right, preferred_element_type=F32)


def dot_tn(left, right):
    return lax.dot_general(left, right, (((0,), (0,)), ((), ())), preferred_element_type=F32)


def dot_nt(left, right):
    return lax.dot_general(left, right, (((1,), (1,)), ((), ())), preferred_element_type=F32)


def shape(*dims, dtype=BF16):
    return jax.ShapeDtypeStruct(dims, dtype)


def in_hbm(value):
    return pltpu.with_memory_space_constraint(value, pltpu.HBM)


def cost(flops, size):
    return pl.CostEstimate(flops=flops, bytes_accessed=size, transcendentals=0)


class Place:
    def __init__(self):
        self.dom = lax.axis_index("dom")
        self.core = lax.axis_index("batch")
        self.at = (self.dom // 16, (self.dom // 4) % 4, self.dom % 4)

    def peer(self, axis, k):
        spot = (self.at[axis] + k) % 4
        return (self.dom + (spot - self.at[axis]) * (16, 4, 1)[axis], self.core), spot

    def across(self, first, second, k):
        spot, spot2 = (self.at[first] + k // 4) % 4, (self.at[second] + k % 4) % 4
        step = (spot - self.at[first]) * (16, 4, 1)[first] + (spot2 - self.at[second]) * (16, 4, 1)[second]
        return (self.dom + step, self.core), spot, spot2


def remote(src, dst, send, recv, device):
    copy = pltpu.make_async_remote_copy(
        src_ref=src, dst_ref=dst, send_sem=send, recv_sem=recv, device_id=device, device_id_type=MESH
    )
    copy.start()
    return copy


def greet(devices):
    barrier = pltpu.get_barrier_semaphore()
    for device in devices:
        pl.semaphore_signal(barrier, inc=1, device_id=device, device_id_type=MESH)
    return lambda: pl.semaphore_wait(barrier, len(devices))


def local_copy(src, dst, sem):
    copy = pltpu.make_async_copy(src, dst, sem)
    copy.start()
    return copy


def upright(row):
    return jnp.broadcast_to(row, (128, N)).T[:, :1]


def front_kernel(
    nexts_in, prevs_in, row_in, x_in, ct_in,
    lab_row, count, most, sums, low, head, got_prev, got_next,
    nexts, prevs, row_ref, x_ref, ct_ref, to_next, to_prev, table, held, rank, peak, peaks,
    load_sem, halo_send, halo_recv, peak_send, peak_recv, head_send, head_recv,
):
    here = Place()
    pair = (here.dom + 1 - 2 * (here.dom % 2), here.core)
    nxt = ((here.dom + 1) % 64, here.core)
    prv = ((here.dom + 63) % 64, here.core)
    loads = [
        local_copy(src, dst, load_sem.at[i])
        for i, (src, dst) in enumerate(
            ((nexts_in, nexts), (prevs_in, prevs), (x_in, x_ref), (row_in, row_ref), (ct_in, ct_ref))
        )
    ]
    wait = greet([nxt, prv] + [here.peer(a, k)[0] for a in range(3) for k in (1, 2, 3)])
    for copy in loads[:3]:
        copy.wait()
    halo = []

    def take(s):
        for j in range(2):
            to_next[s, j] = x_ref[s, nexts[j]]
            to_prev[s, j] = x_ref[s, prevs[j]]

    def ship(s):
        halo.append(remote(to_next.at[s], got_prev.at[s], halo_send.at[0, s], halo_recv.at[0, s], nxt))
        halo.append(remote(to_prev.at[s], got_next.at[s], halo_send.at[1, s], halo_recv.at[1, s], prv))

    take(0)
    wait()
    ship(0)
    take(1)
    ship(1)
    loads[3].wait()
    row = row_ref[...]
    step = 128
    blocks = N // step

    def span(i):
        return pl.ds(pl.multiple_of(i * step, step), step)

    def downs(i):
        return lax.broadcasted_iota(jnp.int32, (step, N), 0) + i * step

    def wide(value):
        return jnp.broadcast_to(jnp.sum(value, axis=1, keepdims=True), (step, 128))

    def holding(i, carry):
        held[span(i), :] = wide(jnp.where(row == downs(i), 1.0, 0.0))
        return carry

    lax.fori_loop(0, blocks, holding, 0)
    held_row = held[...].T[:1]
    total = jnp.sum(jnp.where(held_row == 1.0, 1.0, 0.0), axis=1, keepdims=True)
    count[...] = jnp.broadcast_to(total, (8, 128)).astype(jnp.int32)
    peak[0] = jnp.broadcast_to(total, (8, 128))

    def spread(a):
        return [
            remote(peak.at[a], peaks.at[a, k - 1], peak_send.at[a, k - 1], peak_recv.at[a, k - 1], here.peer(a, k)[0])
            for k in (1, 2, 3)
        ]

    def settle(a, copies):
        for copy in copies:
            copy.wait()
        top = peak[a]
        for k in range(3):
            top = jnp.maximum(top, peaks[a, k])
        return top

    first = spread(0)
    both = jnp.where(held_row == 1.0, 1.0, jnp.where(held_row == 2.0, 2048.0, 0.0))

    def ranking(i, carry):
        across = lax.broadcasted_iota(jnp.int32, (step, N), 1)
        rank[span(i), :] = wide(jnp.where(across < downs(i), both, 0.0))
        return carry

    lax.fori_loop(0, blocks, ranking, 0)
    ranks = rank[:, :1].astype(jnp.int32)
    whole = total.astype(jnp.int32) + (ranks >> 11)
    rank[...] = jnp.broadcast_to(jnp.where(held[:, :1] == 1.0, ranks & 2047, whole), (N, 128)).astype(F32)

    def naming(i, carry):
        mine = jnp.where(row == downs(i), rank[span(i), :1], 0.0)
        return carry + jnp.sum(mine, axis=0, keepdims=True)

    label = lax.fori_loop(0, blocks, naming, jnp.zeros((1, N), F32)).astype(jnp.int32)
    lab_row[...] = label

    def one_hot(i, carry):
        table[span(i), :] = (label == downs(i)).astype(F32).astype(BF16)
        return carry

    lax.fori_loop(0, blocks, one_hot, 0)
    peak[1] = settle(0, first)
    second = spread(1)
    loads[4].wait()

    def pool(s):
        got = dot(table[...], ct_ref[s]).astype(BF16)
        sums[s] = got
        low[s] = got[HEAD:LOW]
        halo.append(remote(sums.at[s, pl.ds(0, HEAD)], head.at[s], head_send.at[s], head_recv.at[s], pair))

    pool(0)
    peak[2] = settle(1, second)
    third = spread(2)
    pool(1)
    most[...] = settle(2, third).astype(jnp.int32)
    for copy in halo:
        copy.wait()

    @pl.when(here.dom == 0)
    def _():
        got_prev[...] = jnp.zeros_like(got_prev)

    @pl.when(here.dom == 63)
    def _():
        got_next[...] = jnp.zeros_like(got_next)


def front(send_next, send_prev, cluster, features, cotangent):
    halo = (SIDE, 2, BLK, D)
    return pl.pallas_call(
        front_kernel,
        out_shape=(
            shape(1, N, dtype=jnp.int32),
            shape(8, 128, dtype=jnp.int32),
            shape(8, 128, dtype=jnp.int32),
            shape(SIDE, N, D),
            shape(SIDE, LOW - HEAD, D),
            shape(SIDE, HEAD, D),
            shape(*halo),
            shape(*halo),
        ),
        in_specs=[HB] * 5,
        out_specs=(VM,) * 8,
        scratch_shapes=[
            pltpu.SMEM((2,), jnp.int32),
            pltpu.SMEM((2,), jnp.int32),
            pltpu.VMEM((1, N), jnp.int32),
            pltpu.VMEM((SIDE, NB, BLK, D), BF16),
            pltpu.VMEM((SIDE, N, D), BF16),
            pltpu.VMEM(halo, BF16),
            pltpu.VMEM(halo, BF16),
            pltpu.VMEM((N, N), BF16),
            pltpu.VMEM((N, 128), F32),
            pltpu.VMEM((N, 128), F32),
            pltpu.VMEM((3, 8, 128), F32),
            pltpu.VMEM((3, 3, 8, 128), F32),
            pltpu.SemaphoreType.DMA((5,)),
            pltpu.SemaphoreType.DMA((2, SIDE)),
            pltpu.SemaphoreType.DMA((2, SIDE)),
            pltpu.SemaphoreType.DMA((3, 3)),
            pltpu.SemaphoreType.DMA((3, 3)),
            pltpu.SemaphoreType.DMA((SIDE,)),
            pltpu.SemaphoreType.DMA((SIDE,)),
        ],
        compiler_params=pltpu.CompilerParams(
            collective_id=0, has_side_effects=True, vmem_limit_bytes=24 * 2**20
        ),
        cost_estimate=cost(4 * 2**30, 2**22),
    )(
        in_hbm(send_next), in_hbm(send_prev), in_hbm(cluster.reshape(1, N)),
        in_hbm(features.reshape(SIDE, NB, BLK, D)), in_hbm(cotangent),
    )


def node_kernel(
    rows, cols, lab_row, x_ref, prev_ref, next_ref, tiles, w_self, w_neigh,
    agg_out, hidden_out, slope_out, sums_out, agg, hidden, slope, sums, ext, acc, table, sem,
):
    for s in range(SIDE):
        span = slice(s * D, (s + 1) * D)
        ext[0:NB, :, span] = x_ref[s].reshape(NB, BLK, D)
        ext[NB : NB + 2, :, span] = prev_ref[s]
        ext[NB + 2 : NB + 4, :, span] = next_ref[s]
    acc[...] = jnp.zeros_like(acc)

    def tile(t, carry):
        r = rows[t]
        acc[r] = acc[r] + dot(tiles[t], ext[cols[t]])
        return carry

    lax.fori_loop(0, tiles.shape[0], tile, 0, unroll=8)
    step = 256

    def block(i, carry):
        at = pl.ds(pl.multiple_of(i * step, step), step)
        down = lax.broadcasted_iota(jnp.int32, (step, N), 0) + i * step
        table[at, :] = (lab_row[...] == down).astype(F32).astype(BF16)
        for s in range(SIDE):
            span = slice(s * D, (s + 1) * D)
            got = acc[pl.ds(i * 2, 2), :, span].reshape(step, D).astype(BF16)
            agg[s, at, :] = got
            pre = dot(x_ref[s, at, :], w_self[...]) + dot(got, w_neigh[...])
            value, grad = silu_pair(pre)
            hidden[s, at, :] = value.astype(BF16)
            slope[s, at, :] = grad.astype(BF16)
        return carry

    lax.fori_loop(0, N // step, block, 0)
    copies = [
        local_copy(src, dst, sem.at[i])
        for i, (src, dst) in enumerate(((agg, agg_out), (hidden, hidden_out), (slope, slope_out)))
    ]
    for s in range(SIDE):
        sums[s] = dot(table[...], hidden[s]).astype(BF16)
        copies.append(local_copy(sums.at[s], sums_out.at[s], sem.at[3 + s]))
    for copy in copies:
        copy.wait()


def node_step(tile_row, tile_col, lab_row, features, got_prev, got_next, tiles, w_self, w_neigh):
    full = pltpu.HBM((SIDE, N, D), BF16)
    return pl.pallas_call(
        node_kernel,
        out_shape=(full,) * 4,
        in_specs=[SM, SM] + [VM] * 7,
        out_specs=(HB,) * 4,
        scratch_shapes=[
            pltpu.VMEM((SIDE, N, D), BF16),
            pltpu.VMEM((SIDE, N, D), BF16),
            pltpu.VMEM((SIDE, N, D), BF16),
            pltpu.VMEM((SIDE, N, D), BF16),
            pltpu.VMEM((NB + 4, BLK, SIDE * D), BF16),
            pltpu.VMEM((NB, BLK, SIDE * D), F32),
            pltpu.VMEM((N, N), BF16),
            pltpu.SemaphoreType.DMA((5,)),
        ],
        compiler_params=pltpu.CompilerParams(vmem_limit_bytes=34 * 2**20),
        cost_estimate=cost(10 * 2**30, 2**23),
    )(tile_row, tile_col, lab_row, features, got_prev, got_next, tiles, w_self, w_neigh)


EARLY = (640, 1024)
CHUNKS = (((0, 384), (384, 640)), ((0, 256), (256, 384), (384, 640)))
ORDERS = ((0, 1, 2), (1, 2, 0), (2, 0, 1))
LATE = CHUNKS[1][-1][1] - CHUNKS[1][-1][0]
ENTRY = (2, 0, 1)
FARTHEST = sorted(range(1, 16), key=lambda k: -min(k // 4, 4 - k // 4) - min(k % 4, 4 - k % 4))


def back_kernel(
    count, lab_row, w_coarse, sums_h_in, sums_c_in, head_in, rec_c_in, far_h_in, far_c_in, x_in, agg_in,
    ct_in, slope_in, hidden_in,
    total, out,
    sums_h, sums_c, rec_c, far_h, far_c, x_ref, agg, ct_ref, slope, hidden, load_sem,
    rec_h, flip, lifted, down, coarse, weighed, x_turn, a_turn, w_turn, grad_pre, part0, part, x_last, a_last, slope_last, grads,
    send0, recv0, acc, buf1, recv1, sum2, buf2, recv2,
    swap_send, swap_recv, send_sem, recv_sem, plane_send, plane_recv, side_send, side_recv,
):
    here = Place()
    core = here.core
    other = (here.dom, 1 - core)
    pair = (here.dom + 1 - 2 * (here.dom % 2), core)
    wait = greet([other, pair] + [here.peer(a, k)[0] for a in range(3) for k in (1, 2, 3)])
    wait()
    swaps, loads = [], []
    for s in range(SIDE):
        for i, (lo, hi) in enumerate(CHUNKS[s]):
            rows = pl.ds(lo, min(hi, LOW) - lo)
            swaps.append(
                remote(sums_h_in.at[s, rows], rec_h.at[s, rows], swap_send.at[s, i], swap_recv.at[s, i], pair)
            )

    for i, (src, dst) in enumerate(
        (
            (sums_h_in, sums_h), (sums_c_in, sums_c), (far_h_in, far_h), (far_c_in, far_c),
            (head_in, rec_c.at[:, pl.ds(0, HEAD)]), (rec_c_in, rec_c.at[:, pl.ds(HEAD, LOW - HEAD)]),
            (x_in, x_ref), (agg_in, agg), (ct_in, ct_ref), (slope_in, slope), (hidden_in, hidden),
        )
    ):
        loads.append(local_copy(src, dst, load_sem.at[i]))
    label = upright(lab_row[...].astype(F32)).astype(jnp.int32)
    across = lax.broadcasted_iota(jnp.int32, (128, N), 1)
    for i in range(0, N, 128):
        flip[i : i + 128, :] = (label[i : i + 128] == across).astype(F32).astype(BF16)
    w_turn[...] = w_coarse[...].T
    for copy in loads[:6]:
        copy.wait()

    def level(s, span, came=True):
        lo, hi = span
        shared = lax.broadcasted_iota(jnp.int32, (hi - lo, 1), 0) + lo < count[0:1, 0:1]

        def joined(own, rec, far):
            if not came:
                return own[s, lo:hi].astype(F32)
            if lo >= LOW:
                got = far[s, lo - LOW : hi - LOW]
            elif hi <= LOW:
                got = rec[s, lo:hi]
            else:
                got = jnp.concatenate([rec[s, lo:LOW], far[s, : hi - LOW]], axis=0)
            return own[s, lo:hi].astype(F32) + jnp.where(shared, got.astype(F32), 0.0)

        rows = (0.5 * joined(sums_h, rec_h, far_h)).astype(BF16)
        coarse[s, lo:hi] = rows
        value, grad = silu_pair(dot(rows, w_coarse[...]))
        lifted[s, lo:hi] = value.astype(BF16)
        grad_act = (joined(sums_c, rec_c, far_c) * grad).astype(BF16)
        below = dot(grad_act, w_turn[...])
        if not came:
            below = jnp.where(shared, 0.0, below)
        down[s, lo:hi] = below.astype(BF16)
        weighed[s, lo:hi] = (grad_act.astype(F32) * jnp.where(shared, 0.5, 1.0)).astype(BF16)

    def looked(s, span):
        lo, hi = span
        return dot(flip[:, lo:hi], down[s, lo:hi])

    def product(s, span):
        lo, hi = span
        return dot_tn(coarse[s, lo:hi], weighed[s, lo:hi])

    def emit(s, lo, hi):
        out[s, lo:hi] = (hidden[s, lo:hi].astype(F32) + dot(flip[lo:hi, :], lifted[s])).astype(BF16)

    def store(p, value):
        grads[p] = value.reshape(2, 4, 4, 16, D)

    def load(p):
        return grads[p].reshape(D, D)

    for s in range(SIDE):
        level(s, EARLY)
    for copy in loads[6:]:
        copy.wait()
    for s in range(SIDE):
        x_turn[s] = x_ref[s].T
        a_turn[s] = agg[s].T

    part0[...] = looked(0, EARLY)
    part[...] = looked(1, EARLY)
    store(2, product(0, EARLY) + product(1, EARLY))
    LAST = CHUNKS[1][-1]
    level(1, LAST, False)
    part[...] += looked(1, LAST)
    late = flip[:, LAST[0] : LAST[1]]
    x_last[...] = dot(x_turn[1], late).astype(BF16)
    a_last[...] = dot(a_turn[1], late).astype(BF16)
    slope_last[...] = dot_tn(late, slope[1]).astype(BF16)

    for i, span in enumerate(CHUNKS[0]):
        swaps[i].wait_recv()
        level(0, span)
        part0[...] += looked(0, span)
        store(2, load(2) + product(0, span))
    grad_pre[...] = ((ct_ref[0].astype(F32) + 0.5 * part0[...]) * slope[0].astype(F32)).astype(BF16)
    store(0, dot(x_turn[0], grad_pre[...]))
    store(1, dot(a_turn[0], grad_pre[...]))
    for i, span in enumerate(CHUNKS[1][:-1]):
        swaps[2 + i].wait_recv()
        level(1, span)
        part[...] += looked(1, span)
        store(2, load(2) + product(1, span))
    grad_pre[...] = ((ct_ref[1].astype(F32) + 0.5 * part[...]) * slope[1].astype(F32)).astype(BF16)
    store(0, load(0) + dot(x_turn[1], grad_pre[...]))
    store(1, load(1) + dot(a_turn[1], grad_pre[...]))
    swaps[4].wait_recv()
    level(1, LAST)
    first = [None] * 3

    def hand(p):
        send0[p] = grads[p, 1 - core].astype(BF16)
        first[p] = remote(send0.at[p], recv0.at[p], side_send.at[0, p], side_recv.at[0, p], other)

    store(2, load(2) + product(1, LAST))
    hand(2)
    split = lax.broadcasted_iota(jnp.int32, (LAST[1] - LAST[0], 1), 0) + LAST[0] < count[0:1, 0:1]
    below = jnp.where(split, 0.5 * down[1, LAST[0] : LAST[1]].astype(F32), 0.0)
    grad_last = (below * slope_last[...].astype(F32)).astype(BF16)
    store(0, load(0) + dot(x_last[...], grad_last))
    hand(0)
    store(1, load(1) + dot(a_last[...], grad_last))
    hand(1)

    def mine(p):
        return [here.at[axis] for axis in ORDERS[p]]

    def cols(spot):
        return pl.ds(pl.multiple_of(spot * 128, 128), 128)

    stages = [[None] * 3 for _ in range(4)]

    def arrived(stage, p):
        for copy in stages[stage][p]:
            copy.wait_recv()

    for p in ENTRY:
        first[p].wait_recv()
        value = grads[p, core] + recv0[p].astype(F32)
        acc[p] = value
        buf1[p] = value.astype(BF16)
        stages[0][p] = []
        for k in (2, 1, 3):
            device, spot = here.peer(ORDERS[p][0], k)
            stages[0][p].append(
                remote(buf1.at[p, spot], recv1.at[p, k - 1], send_sem.at[0, p, k - 1], recv_sem.at[0, p, k - 1], device)
            )
    emit(0, 0, N)
    for p in ENTRY:
        arrived(0, p)
        value = acc[p, mine(p)[0]]
        for k in range(3):
            value = value + recv1[p, k].astype(F32)
        sum2[p] = value
        buf2[p] = value.astype(BF16)
    for p in ENTRY:
        stages[1][p] = []
        for k in FARTHEST:
            device, spot, spot2 = here.across(ORDERS[p][1], ORDERS[p][2], k)
            stages[1][p].append(
                remote(
                    buf2.at[p, spot, :, cols(spot2)], recv2.at[p, k - 1],
                    plane_send.at[0, p, k - 1], plane_recv.at[0, p, k - 1], device,
                )
            )
    emit(1, 0, 512)
    for p in ENTRY:
        arrived(1, p)
        one, two, three = mine(p)
        value = sum2[p, two, :, cols(three)]
        for k in range(15):
            value = value + recv2[p, k].astype(F32)
        piece = total.at[p, core, one, two, :, cols(three)]
        piece[...] = value.astype(BF16)
        stages[2][p] = []
        for k in FARTHEST:
            device, _, _ = here.across(ORDERS[p][1], ORDERS[p][2], k)
            stages[2][p].append(
                remote(piece, piece, plane_send.at[1, p, k - 1], plane_recv.at[1, p, k - 1], device)
            )
    emit(1, 512, N)
    for p in ENTRY:
        arrived(2, p)
        piece = total.at[p, core, mine(p)[0]]
        stages[3][p] = []
        for k in (2, 1, 3):
            device, _ = here.peer(ORDERS[p][0], k)
            stages[3][p].append(
                remote(piece, piece, send_sem.at[1, p, k - 1], recv_sem.at[1, p, k - 1], device)
            )
    last = []
    for p in ENTRY:
        arrived(3, p)
        last.append(remote(total.at[p, core], total.at[p, core], side_send.at[1, p], side_recv.at[1, p], other))
    for copy in last:
        copy.wait_recv()
    for group in stages:
        for copies in group:
            for copy in copies:
                copy.wait_send()
    for copy in swaps + first + last:
        copy.wait_send()


def back_step(*args):
    half = (3, 4, 4, 16, D)
    return pl.pallas_call(
        back_kernel,
        out_shape=(shape(3, 2, 4, 4, 16, D), shape(SIDE, N, D)),
        in_specs=[VM] * 3 + [HB] * (len(args) - 3),
        out_specs=(VM, VM),
        scratch_shapes=[
            pltpu.VMEM((SIDE, N, D), BF16),
            pltpu.VMEM((SIDE, N, D), BF16),
            pltpu.VMEM((SIDE, LOW, D), BF16),
            pltpu.VMEM((SIDE, N - LOW, D), BF16),
            pltpu.VMEM((SIDE, N - LOW, D), BF16),
            pltpu.VMEM((SIDE, N, D), BF16),
            pltpu.VMEM((SIDE, N, D), BF16),
            pltpu.VMEM((SIDE, N, D), BF16),
            pltpu.VMEM((SIDE, N, D), BF16),
            pltpu.VMEM((SIDE, N, D), BF16),
            pltpu.SemaphoreType.DMA((11,)),
            pltpu.VMEM((SIDE, LOW, D), BF16),
            pltpu.VMEM((N, N), BF16),
            pltpu.VMEM((SIDE, N, D), BF16),
            pltpu.VMEM((SIDE, N, D), BF16),
            pltpu.VMEM((SIDE, N, D), BF16),
            pltpu.VMEM((SIDE, N, D), BF16),
            pltpu.VMEM((SIDE, D, N), BF16),
            pltpu.VMEM((SIDE, D, N), BF16),
            pltpu.VMEM((D, D), BF16),
            pltpu.VMEM((N, D), BF16),
            pltpu.VMEM((N, D), F32),
            pltpu.VMEM((N, D), F32),
            pltpu.VMEM((D, LATE), BF16),
            pltpu.VMEM((D, LATE), BF16),
            pltpu.VMEM((LATE, D), BF16),
            pltpu.VMEM((3, 2, 4, 4, 16, D), F32),
            pltpu.VMEM(half, BF16),
            pltpu.VMEM(half, BF16),
            pltpu.VMEM(half, F32),
            pltpu.VMEM(half, BF16),
            pltpu.VMEM((3, 3, 4, 16, D), BF16),
            pltpu.VMEM((3, 4, 16, D), F32),
            pltpu.VMEM((3, 4, 16, D), BF16),
            pltpu.VMEM((3, 15, 16, 128), BF16),
            pltpu.SemaphoreType.DMA((SIDE, 3)),
            pltpu.SemaphoreType.DMA((SIDE, 3)),
            pltpu.SemaphoreType.DMA((2, 3, 3)),
            pltpu.SemaphoreType.DMA((2, 3, 3)),
            pltpu.SemaphoreType.DMA((2, 3, 15)),
            pltpu.SemaphoreType.DMA((2, 3, 15)),
            pltpu.SemaphoreType.DMA((2, 3)),
            pltpu.SemaphoreType.DMA((2, 3)),
        ],
        compiler_params=pltpu.CompilerParams(
            collective_id=1, has_side_effects=True, vmem_limit_bytes=48 * 2**20
        ),
        cost_estimate=cost(12 * 2**30, 2**24),
    )(*args[:3], *(in_hbm(arg) for arg in args[3:]))


def close_kernel(scale, total, out_in, out, g0, g1, g2, wide, sem):
    copies = [local_copy(out_in.at[s], out.at[s], sem.at[3 + s]) for s in range(SIDE)]
    for p, g in enumerate((g0, g1, g2)):
        wide[p] = total[p].astype(F32) * scale
        copies.append(local_copy(wide.at[p], g, sem.at[p]))
    for copy in copies:
        copy.wait()


def close(scale, total, out):
    return pl.pallas_call(
        functools.partial(close_kernel, scale),
        out_shape=(shape(SIDE, N, D),) + (shape(D, D, dtype=F32),) * 3,
        in_specs=[VM, VM],
        out_specs=(HB,) * 4,
        scratch_shapes=[pltpu.VMEM((3, D, D), F32), pltpu.SemaphoreType.DMA((5,))],
        compiler_params=pltpu.CompilerParams(vmem_limit_bytes=8 * 2**20),
    )(total, out)


def local(
    features,
    tile_vals,
    tile_row,
    tile_col,
    send_next,
    send_prev,
    cluster,
    cotangent,
    self_weight,
    neighbour_weight,
    w_coarse,
):
    lab_row, count, most, sums_c, low_c, head_c, got_prev, got_next = front(
        send_next, send_prev, cluster, features, cotangent
    )
    rec_c = partner(low_c)
    agg, hidden, slope, sums_h = node_step(
        tile_row, tile_col, lab_row, features, got_prev, got_next, tile_vals,
        self_weight, neighbour_weight,
    )
    far_h, far_c = lax.cond(
        most[0, 0] > LOW,
        lambda h, c: (partner(h[:, LOW:]), partner(c[:, LOW:])),
        lambda h, c: (jnp.zeros((SIDE, N - LOW, D), BF16),) * 2,
        sums_h,
        sums_c,
    )
    total, output = back_step(
        count, lab_row, w_coarse, sums_h, sums_c, head_c, rec_c, far_h, far_c, features, agg, cotangent, slope,
        hidden,
    )
    scale = 1.0 / math.sqrt(SIDE * lax.axis_size("batch") * N * lax.axis_size("dom"))
    return close(scale, total.reshape(3, D, D), output)


def solution(mesh):
    in_specs = (
        P("batch", "dom", None),
        P("dom", None, None),
        P("dom"),
        P("dom"),
        P("dom"),
        P("dom"),
        P("dom"),
        P("batch", "dom", None),
        P(),
        P(),
        P(),
    )
    out_specs = (P("batch", "dom", None), P(), P(), P())
    return jax.shard_map(local, mesh=mesh, in_specs=in_specs, out_specs=out_specs, check_vma=False)
```
